32 devices in a mesh: row: 16 (over z, x, core), grp: 2 (over y).
Axes of the slice: x: 2, y: 2, z: 4, core: 2. Of those that a mesh axis runs over, the one named last changes fastest.
Arguments:
- panel_rows: bfloat16 [16384, 1024], P(('row', 'grp')), may hold values from -300 to 300, as said below
- sign_bits: int32 [16384], P(('row', 'grp')), may hold values from 0 to 1
- sample_rows: int32 [8192], replicated, may hold values from 0 to 16383, as said below
Outputs:
- factor: float32 [1024, 1024], P('row', 'grp')
The draws below stay inside these ranges and needn't reach their ends.
Inputs may be any that keep to these rules, and one draw needn't show every extreme that they name: `sample_rows`: distinct and ascending. Each aligned block of 512 rows (the rows of one device) holds at most 512 sampled rows, and at least a quarter of these blocks hold exactly 512. `panel_rows`: finite values.
All inputs are finite; a program needn't handle non-finite values.
Results may differ from the reference program's by a relative error of at most 0.0011.
Values may be sent and summed in bfloat16 or wider, within the bound.
No kernel may reach another device: no remote copies, remote signals or barrier semaphores. Data moves between devices by JAX's collectives and lax.ppermute only.
A program may use at most 64 MiB of HBM per device.

```python
import math
import jax
import jax.numpy as jnp
from jax import lax

COLS = 1024
ROWS_DEV = 512
NS = 8192
NBLK = 32
ROWS = 16384
SAMP_DEV = 256
CAP = 512
N_ROW = 16
N_GRP = 2


def draw_panel_rows(key, part):
    total_rows = ROWS_DEV * NBLK
    keys = jax.random.split(jax.random.fold_in(key, 11), 3)
    base_vals = jax.random.normal(keys[0], (total_rows, COLS), jnp.float32)
    row_scale = jnp.exp(jax.random.uniform(keys[1], (total_rows, 1), jnp.float32, math.log(0.5), math.log(5.0)))
    col_scale = jnp.exp(jax.random.uniform(keys[2], (1, COLS), jnp.float32, math.log(0.5), math.log(5.0)))
    return jnp.clip(base_vals * row_scale * col_scale, -300.0, 300.0).astype(jnp.bfloat16)


def draw_sample_rows(key, part):
    keys = jax.random.split(jax.random.fold_in(key, 23), 4)
    groups = NBLK // 4
    first_count = jax.random.randint(keys[0], (groups,), 0, 2 * SAMP_DEV + 1)
    second_count = jax.random.randint(keys[1], (groups,), 0, 2 * SAMP_DEV + 1 - first_count)
    third_count = 2 * SAMP_DEV - first_count - second_count
    counts = jnp.stack([jnp.full((groups,), CAP, jnp.int32), first_count, second_count, third_count], 1).reshape(NBLK)
    counts = counts[jax.random.permutation(keys[2], NBLK)]
    row_keys = jax.random.split(keys[3], NBLK)
    perms = jax.vmap(lambda row_key: jax.random.permutation(row_key, ROWS_DEV))(row_keys)
    ranks = jnp.argsort(perms, axis=1, stable=True).astype(jnp.int32)
    chosen = (ranks < counts[:, None]).reshape(-1)
    return jnp.nonzero(chosen, size=NS, fill_value=0)[0].astype(jnp.int32)


def with_ends(result, rng, smallest, high):
    dims = result.shape
    place = [jax.random.randint(jax.random.fold_in(rng, axis), (), 0, dims[axis]) for axis in range(len(dims))]
    result = result.at[tuple(place)].set(smallest)
    longest = dims.index(max(dims))
    place[longest] = (place[longest] + 1) % dims[longest]
    return result.at[tuple(place)].set(high)


def setup_inputs(seed: int = 0) -> dict:
    key_list = jax.random.split(jax.random.key(seed), 4)
    return {
        "panel_rows": draw_panel_rows(jax.random.fold_in(key_list[3], 71), 0),
        "sign_bits": with_ends(jax.random.randint(key_list[1], (ROWS,), 0, 2), jax.random.fold_in(key_list[1], 1), 0, 1).astype(jnp.int32),
        "sample_rows": draw_sample_rows(jax.random.fold_in(key_list[3], 71), 0),
    }


def hadamard(table_size):
    row_ids = lax.broadcasted_iota(jnp.int32, (table_size, table_size), 0)
    col_ids = lax.broadcasted_iota(jnp.int32, (table_size, table_size), 1)
    shared = row_ids & col_ids
    parity = jnp.zeros((table_size, table_size), jnp.int32)
    for bit_pos in range(table_size.bit_length() - 1):
        parity = parity ^ shared >> bit_pos & 1
    return (1 - 2 * parity).astype(jnp.float32)

def reference(panel_rows, sign_bits, sample_rows):
    flipped = panel_rows.astype(jnp.float32) * (1 - 2 * sign_bits).astype(jnp.float32)[:, None]
    blocks = flipped.reshape(N_ROW, N_GRP, ROWS_DEV, COLS)
    blocks = jnp.einsum('ar,rglc->aglc', hadamard(N_ROW), blocks, precision=lax.Precision.HIGHEST)
    blocks = jnp.einsum('bg,aglc->ablc', hadamard(N_GRP), blocks, precision=lax.Precision.HIGHEST)
    by_device = blocks.reshape(N_ROW * N_GRP, ROWS_DEV, COLS)
    local_table = hadamard(ROWS_DEV)
    norm_scale = 1.0 / math.sqrt(ROWS_DEV * N_ROW * N_GRP * NS)

    def one_block(sample_ids):
        device_ids = (sample_ids // ROWS_DEV).astype(jnp.int32)
        local_ids = (sample_ids % ROWS_DEV).astype(jnp.int32)
        table_rows = local_table[local_ids]
        source = by_device[device_ids]
        summed = jnp.einsum('sk,skc->sc', table_rows, source, precision=lax.Precision.HIGHEST)
        return (summed * norm_scale).astype(jnp.bfloat16)
    sketch = lax.map(one_block, sample_rows.reshape(-1, 64)).reshape(NS, COLS)
    gram_matrix = jnp.dot(sketch.T.astype(jnp.float32), sketch.astype(jnp.float32), preferred_element_type=jnp.float32)
    return jnp.linalg.cholesky(gram_matrix)
```

```python
import functools
import math

import jax
import jax.numpy as jnp
from jax import lax
from jax.experimental import pallas as pl
from jax.experimental.pallas import tpu as pltpu
from jax.sharding import PartitionSpec as P

AXES = ("row", "grp")
TILE = 128
f32 = jnp.float32
HI = lax.Precision.HIGHEST


def hadamard(table_size, dtype):
    row_ids = lax.broadcasted_iota(jnp.int32, (table_size, table_size), 0)
    col_ids = lax.broadcasted_iota(jnp.int32, (table_size, table_size), 1)
    shared = row_ids & col_ids
    parity = jnp.zeros((table_size, table_size), jnp.int32)
    for bit_pos in range(table_size.bit_length() - 1):
        parity = parity ^ shared >> bit_pos & 1
    return (1 - 2 * parity).astype(dtype)


def mix_lead(exchanged):
    lead_table = hadamard(exchanged.shape[0], jnp.float32)
    return jnp.einsum("ab,bic->aic", lead_table, exchanged, precision=lax.Precision.HIGHEST)


def mix_grp(exchanged):
    return lax.all_to_all(mix_lead(exchanged), "grp", split_axis=0, concat_axis=2, tiled=True)


def local_plain(panel_rows, sign_bits, sample_rows):
    rows_dev, n_cols = panel_rows.shape
    n_row = lax.axis_size("row")
    n_grp = lax.axis_size("grp")
    flipped = panel_rows * (1 - 2 * sign_bits).astype(jnp.bfloat16)[:, None]
    local_table = hadamard(rows_dev, jnp.bfloat16)
    local_mix = jnp.dot(local_table, flipped, preferred_element_type=jnp.float32)
    grp_mixed = mix_grp(
        lax.all_to_all(local_mix[None], "grp", split_axis=2, concat_axis=0, tiled=True)
    )
    num_samples = sample_rows.shape[0]
    total_rows = rows_dev * n_row * n_grp
    norm_scale = 1.0 / math.sqrt(total_rows * num_samples)
    col_width = n_cols // n_grp
    col_start = lax.axis_index("grp") * col_width
    held = mix_lead(lax.all_to_all(grp_mixed, "row", split_axis=1, concat_axis=0, tiled=True))
    slice_width = held.shape[1]
    block_pos = lax.broadcasted_iota(jnp.int32, (n_row, slice_width), 0)
    inner_pos = lax.broadcasted_iota(jnp.int32, (n_row, slice_width), 1)
    held_ids = (
        (block_pos * n_grp + lax.axis_index("grp")) * rows_dev
        + lax.axis_index("row") * slice_width
        + inner_pos
    ).reshape(-1)
    found_pos = jnp.clip(jnp.searchsorted(sample_rows, held_ids), 0, num_samples - 1)
    is_sampled = jnp.take(sample_rows, found_pos) == held_ids
    held_flat = held.reshape(n_row * slice_width, n_cols)
    sketch_held = jnp.where(is_sampled[:, None], held_flat * norm_scale, 0.0).astype(jnp.bfloat16)
    shard_rows = lax.all_gather(sketch_held, "grp", axis=0, tiled=True)
    own_cols = lax.dynamic_slice_in_dim(shard_rows, col_start, col_width, 1)
    partial_value = lax.dot_general(
        shard_rows, own_cols, (((0,), (0,)), ((), ())), preferred_element_type=jnp.float32
    )
    gram_block = lax.psum_scatter(partial_value, "row", scatter_dimension=0, tiled=True)
    gathered = lax.all_gather(gram_block[None], ("row", "grp"), axis=0, tiled=True)
    gram_matrix = (
        gathered.reshape(n_row, n_grp, n_cols // n_row, col_width)
        .transpose(0, 2, 1, 3)
        .reshape(n_cols, n_cols)
    )
    lower_factor = jnp.linalg.cholesky(gram_matrix)
    row_width = n_cols // n_row
    return lax.dynamic_slice(
        lower_factor, (lax.axis_index("row") * row_width, col_start), (row_width, col_width)
    )


def mm(a,b,dims=(((1,),(0,)),((),()))):
    return lax.dot_general(a,b,dims,precision=HI,preferred_element_type=f32)
TA=(((0,),(0,)),((),()))
TB=(((1,),(1,)),((),()))

def elim(X, sbase, ibase, n, zero=None):
    G=n//8
    xs=[X[8*g:8*g+8,:] for g in range(G)]
    rid=lax.broadcasted_iota(jnp.int32,(8,128),0)
    full=lambda v: jnp.broadcast_to(v,(8,128))
    out=[]
    for g in range(G):
        C=[[None]*G for _ in range(8)]
        for m in range(8):
            for h in range(g,G):
                l=sbase+8*g+m
                C[m][h]=full(xs[h][:,l:l+1])
        for m in range(8): C[m][g]=C[m][g]+zero
        o=jnp.zeros((8,128),f32)
        for j in range(0,8,2):
            a=full(C[j][g][j:j+1,:]); b=full(C[j][g][j+1:j+2,:]); c=full(C[j+1][g][j+1:j+2,:])
            r0=full(xs[g][j:j+1,:]); r1=full(xs[g][j+1:j+2,:])
            det=a*c-b*b
            inv=1.0/det
            ws=[]
            for m in range(j+2,8):
                q0=full(C[m][g][j:j+1,:]); q1=full(C[m][g][j+1:j+2,:])
                if j==0:
                    q0=q0; q1=q1
                ws.append((m,(c*q0-b*q1)*inv,(a*q1-b*q0)*inv))
            t1=a*r1-b*r0
            u0=(c*r0-b*r1)*inv; u1=t1*inv
            for m,w0,w1 in ws:
                for h in range(g,G):
                    C[m][h]=C[m][h]-C[j][h]*w0-C[j+1][h]*w1
            for h in range(g,G):
                if h>g or j<6:
                    xs[h]=xs[h]-C[j][h]*u0-C[j+1][h]*u1
            l0=r0*lax.rsqrt(a); l1=t1*lax.rsqrt(a*det)
            o=jnp.where(rid==j,l0,jnp.where(rid==j+1,l1,o))
        out.append(o)
    return jnp.concatenate(out,axis=0)

def factor128(D,zero):
    lane=lax.broadcasted_iota(jnp.int32,(64,128),1)
    row=lax.broadcasted_iota(jnp.int32,(64,128),0)
    z=jnp.zeros((64,128),f32)
    def equil(S,off,ioff):
        e=lane==row+off
        dg=jnp.where(e,S,0.0)
        dc=lax.rsqrt(jnp.sum(dg,axis=1,keepdims=True))
        dsum=jnp.sum(dg,axis=0,keepdims=True)
        half=(lane>=off)&(lane<off+64)
        drow=jnp.where(half[0:1],dsum,1.0)
        dr=lax.rsqrt(drow)
        X=jnp.where(half,S*dc*dr,jnp.where(lane==row+ioff,dc,0.0))
        back=jnp.where(half[0:1],drow*dr,1.0)
        return X,back
    Dt=D[:64,:]; Db=D[64:,:]
    X1,bk1=equil(Dt,0,64)
    F1=elim(X1,0,64,64,zero)*bk1
    U1=mm(F1,jnp.concatenate([z,Dt],axis=0))
    U12=jnp.where(lane>=64,U1,0.0)
    T=mm(U12,U12,TA)
    D2=Db-T[64:,:]
    X2,bk2=equil(D2,64,0)
    F2=elim(X2,64,0,64,zero)*bk2
    W1=jnp.where(lane>=64,F1,0.0)
    Q=mm(U12,F1,TA)
    V=mm(F2,jnp.concatenate([Q[64:,:],z],axis=0))
    W1s=pltpu.roll(F1,64,1); Vs=pltpu.roll(V,64,1)
    lo=lane<64
    Wtop=jnp.where(lo,W1s,0.0)
    W2s=pltpu.roll(F2,64,1)
    Wbot=jnp.where(lo,-Vs,W2s)
    Utop=jnp.where(lo,jnp.where(lane>=row,F1,0.0),U1)
    Ubot=jnp.where((~lo)&(lane-64>=row),F2,0.0)
    return jnp.concatenate([Utop,Ubot],axis=0),jnp.concatenate([Wtop,Wbot],axis=0)


def sketch_gram_kernel(n_dev, me_ref, x_ref, m_ref, keep_ref, send_ref, s_ref, fold):
    n = x_ref.shape[2]
    nb = n // TILE
    per = x_ref.shape[1]

    def mix(c, _):
        cols = pl.ds(pl.multiple_of(c * TILE, TILE), TILE)
        for sub in range(per // 8):
            v = [x_ref[b, 8 * sub : 8 * sub + 8, cols] for b in range(n_dev)]
            h = 1
            while h < n_dev:
                w = list(v)
                for b in range(n_dev):
                    if not b & h:
                        w[b] = v[b] + v[b | h]
                        w[b | h] = v[b] - v[b | h]
                v = w
                h *= 2
            for b in range(0, n_dev, 2):
                r = (sub * n_dev + b) * 8
                pair = jnp.concatenate([v[b], v[b + 1]], axis=0) * m_ref[r : r + 16, :]
                s_ref[r : r + 16, cols] = pair.astype(jnp.bfloat16)
        return 0

    lax.fori_loop(0, nb, mix, 0)
    for k in range(nb):
        part = lax.dot_general(
            s_ref[:, k * TILE : (k + 1) * TILE],
            s_ref[:, k * TILE :],
            TA,
            preferred_element_type=f32,
        )
        panel, off = (k, 0) if k < nb // 2 else (nb - 1 - k, k + 1)
        fold[panel * TILE : (panel + 1) * TILE, off * TILE : (off + nb - k) * TILE] = part
    half = n_dev // 2
    me = me_ref[0]
    h = keep_ref.shape[1]

    def put(j, _):
        keep_ref[j] = fold[pl.ds(pl.multiple_of((j ^ me) * h, 8), h), :]
        send_ref[j] = fold[pl.ds(pl.multiple_of(((j + half) ^ me) * h, 8), h), :]
        return 0

    lax.fori_loop(0, half, put, 0)


def factor_kernel(n, pos_ref, own_ref, recv_ref, out_ref, fold, u_ref, strip, zref, turn):
    B = TILE
    nb = n // B
    CW = 2 * B
    half = own_ref.shape[0]
    h = own_ref.shape[1]
    me = pos_ref[0]

    def get(j, _):
        fold[pl.ds(pl.multiple_of((j ^ me) * h, 8), h), :] = own_ref[j]
        fold[pl.ds(pl.multiple_of(((j + half) ^ me) * h, 8), h), :] = recv_ref[j]
        return 0

    lax.fori_loop(0, half, get, 0)
    zref[...] = jnp.zeros((8, 128), f32)

    def body(k, _):
        kc = pl.multiple_of(k * B, B)
        low = k < nb // 2
        panel = jnp.where(low, k, nb - 1 - k)
        off = jnp.where(low, -k, 1)

        def load(c, _):
            src = pl.multiple_of((c + off) * B, B)
            strip[:, pl.ds(pl.multiple_of(c * B, B), B)] = fold[
                pl.ds(pl.multiple_of(panel * B, B), B), pl.ds(src, B)
            ]
            return 0

        lax.fori_loop(k, nb, load, 0)
        c0 = kc // CW
        nc = n // CW

        def chunk(c, _):
            cc = pl.multiple_of(c * CW, CW)

            def kk(j, acc):
                jj = pl.multiple_of(j * B, B)
                return acc + mm(u_ref[pl.ds(jj, B), pl.ds(kc, B)], u_ref[pl.ds(jj, B), pl.ds(cc, CW)], TA)

            acc = lax.fori_loop(0, k, kk, jnp.zeros((B, CW), f32))
            strip[:, pl.ds(cc, CW)] = strip[:, pl.ds(cc, CW)] - acc
            return 0

        lax.fori_loop(c0, nc, chunk, 0)
        U, W = factor128(strip[:, pl.ds(kc, B)], zref[...])

        def pan(c, _):
            cc = pl.multiple_of(c * CW, CW)
            u_ref[pl.ds(kc, B), pl.ds(cc, CW)] = mm(W, strip[:, pl.ds(cc, CW)])
            return 0

        lax.fori_loop(c0, nc, pan, 0)
        u_ref[pl.ds(kc, B), pl.ds(kc, B)] = U
        return 0

    lax.fori_loop(0, nb, body, 0)
    row_width, col_width = out_ref.shape
    first_row = pos_ref[1] * row_width
    first_col = pos_ref[2] * col_width
    lane_tile = pl.multiple_of(first_row // B * B, B)
    inner = pl.multiple_of(first_row % B, 8)
    for c in range(col_width // B):
        block = u_ref[pl.ds(pl.multiple_of(first_col + c * B, B), B), pl.ds(lane_tile, B)]
        turn[...] = block.T
        i = first_row + lax.broadcasted_iota(jnp.int32, (row_width, B), 0)
        j = first_col + c * B + lax.broadcasted_iota(jnp.int32, (row_width, B), 1)
        out_ref[:, c * B : (c + 1) * B] = jnp.where(j <= i, turn[pl.ds(inner, row_width), :], 0.0)


def xor_send(value, mask, n_dev):
    return lax.ppermute(value, AXES, [(d, d ^ mask) for d in range(n_dev)])


def local_fast(panel_rows, sign_bits, sample_rows):
    rows_dev, n = panel_rows.shape
    n_row = lax.axis_size("row")
    n_grp = lax.axis_size("grp")
    n_dev = n_row * n_grp
    per = rows_dev // n_dev
    num_samples = sample_rows.shape[0]
    norm_scale = 1.0 / math.sqrt(rows_dev * n_dev * num_samples)
    row_i = lax.axis_index("row")
    grp_i = lax.axis_index("grp")
    lin = row_i * n_grp + grp_i

    flipped = panel_rows * (1 - 2 * sign_bits).astype(jnp.bfloat16)[:, None]
    local_mix = jnp.dot(hadamard(rows_dev, jnp.bfloat16), flipped, preferred_element_type=f32)
    mixed = lax.all_to_all(local_mix, AXES, split_axis=0, concat_axis=0, tiled=True)
    mixed = mixed.reshape(n_dev, per, n)

    r = lax.iota(jnp.int32, rows_dev)
    held_ids = (r // 8 % n_dev) * rows_dev + lin * per + r // (8 * n_dev) * 8 + r % 8
    is_sampled = jnp.any(held_ids[:, None] == sample_rows[None, :], axis=1)
    weight = jnp.where(is_sampled, norm_scale, 0.0).astype(f32)
    weight = jnp.broadcast_to(weight[:, None], (rows_dev, TILE))

    grp_bits = [1 << b for b in range(n_grp.bit_length() - 1)]
    row_bits = [n_grp << b for b in range(n_row.bit_length() - 1)]
    stages = [row_bits[:1], row_bits[1:2] + grp_bits, row_bits[2:]]
    order = [bit for stage in stages for bit in reversed(stage)]
    place = jnp.int32(0)
    for bit in order:
        place = place * 2 + (lin & bit) // bit

    def mask_of(stage, step):
        return sum(bit for pos, bit in enumerate(stage) if step >> pos & 1)

    nb = n // TILE
    fold_rows = nb // 2 * TILE
    fold_cols = (nb + 1) * TILE
    h = fold_rows // n_dev
    half = n_dev // 2
    piece = jax.ShapeDtypeStruct((half, h, fold_cols), f32)
    vmem = pl.BlockSpec(memory_space=pltpu.VMEM)
    smem = pl.BlockSpec(memory_space=pltpu.SMEM)
    keep, send = pl.pallas_call(
        functools.partial(sketch_gram_kernel, n_dev),
        out_shape=(piece, piece),
        in_specs=[smem, vmem, vmem],
        out_specs=(vmem, vmem),
        scratch_shapes=[pltpu.VMEM((rows_dev, n), jnp.bfloat16), pltpu.VMEM((fold_rows, fold_cols), f32)],
        compiler_params=pltpu.CompilerParams(vmem_limit_bytes=40 << 20),
        name="sketch_gram",
    )(place[None], mixed, weight)

    total = keep + xor_send(send, mask_of(stages[0], 1), n_dev)
    for stage in stages[1:]:
        ways = 1 << len(stage)
        if ways == 1:
            continue
        parts = total.reshape(ways, total.shape[0] // ways, h, fold_cols)
        got = [xor_send(parts[s], mask_of(stage, s), n_dev) for s in range(1, ways)]
        total = parts[0]
        for g in got:
            total = total + g
    for stage in reversed(stages[1:]):
        ways = 1 << len(stage)
        if ways == 1:
            continue
        got = [xor_send(total, mask_of(stage, s), n_dev) for s in range(1, ways)]
        total = jnp.concatenate([total] + got, axis=0)
    other = xor_send(total, mask_of(stages[0], 1), n_dev)

    row_width = n // n_row
    col_width = n // n_grp
    return pl.pallas_call(
        functools.partial(factor_kernel, n),
        out_shape=jax.ShapeDtypeStruct((row_width, col_width), f32),
        in_specs=[smem, vmem, vmem],
        out_specs=vmem,
        scratch_shapes=[
            pltpu.VMEM((fold_rows, fold_cols), f32),
            pltpu.VMEM((n, n), f32),
            pltpu.VMEM((TILE, n), f32),
            pltpu.VMEM((8, 128), f32),
            pltpu.VMEM((TILE, TILE), f32),
        ],
        compiler_params=pltpu.CompilerParams(vmem_limit_bytes=40 << 20),
        name="factor",
    )(jnp.stack([place, row_i, grp_i]), total, other)


def local(panel_rows, sign_bits, sample_rows):
    rows_dev, n = panel_rows.shape
    n_row = lax.axis_size("row")
    n_grp = lax.axis_size("grp")
    n_dev = n_row * n_grp
    fits = (
        n % (2 * TILE) == 0
        and n_dev & (n_dev - 1) == 0
        and 2 <= n_row
        and n_dev <= 64
        and rows_dev % (8 * n_dev) == 0
        and n // 2 % (8 * n_dev) == 0
        and TILE % (n // n_row) == 0
        and n // n_row % 8 == 0
        and n // n_grp % TILE == 0
    )
    return (local_fast if fits else local_plain)(panel_rows, sign_bits, sample_rows)


def solution(mesh):
    return jax.shard_map(
        local,
        mesh=mesh,
        in_specs=(P(("row", "grp"), None), P(("row", "grp")), P()),
        out_specs=P("row", "grp"),
        check_vma=False,
    )
```

```python
import functools
import math

import jax
import jax.numpy as jnp
from jax import lax
from jax.experimental import pallas as pl
from jax.experimental.pallas import tpu as pltpu
from jax.sharding import PartitionSpec as P

AXES = ("row", "grp")
TILE = 128
f32 = jnp.float32
HI = lax.Precision.HIGHEST


def hadamard(table_size, dtype):
    row_ids = lax.broadcasted_iota(jnp.int32, (table_size, table_size), 0)
    col_ids = lax.broadcasted_iota(jnp.int32, (table_size, table_size), 1)
    shared = row_ids & col_ids
    parity = jnp.zeros((table_size, table_size), jnp.int32)
    for bit_pos in range(table_size.bit_length() - 1):
        parity = parity ^ shared >> bit_pos & 1
    return (1 - 2 * parity).astype(dtype)


def mix_lead(exchanged):
    lead_table = hadamard(exchanged.shape[0], jnp.float32)
    return jnp.einsum("ab,bic->aic", lead_table, exchanged, precision=lax.Precision.HIGHEST)


def mix_grp(exchanged):
    return lax.all_to_all(mix_lead(exchanged), "grp", split_axis=0, concat_axis=2, tiled=True)


def local_plain(panel_rows, sign_bits, sample_rows):
    rows_dev, n_cols = panel_rows.shape
    n_row = lax.axis_size("row")
    n_grp = lax.axis_size("grp")
    flipped = panel_rows * (1 - 2 * sign_bits).astype(jnp.bfloat16)[:, None]
    local_table = hadamard(rows_dev, jnp.bfloat16)
    local_mix = jnp.dot(local_table, flipped, preferred_element_type=jnp.float32)
    grp_mixed = mix_grp(
        lax.all_to_all(local_mix[None], "grp", split_axis=2, concat_axis=0, tiled=True)
    )
    num_samples = sample_rows.shape[0]
    total_rows = rows_dev * n_row * n_grp
    norm_scale = 1.0 / math.sqrt(total_rows * num_samples)
    col_width = n_cols // n_grp
    col_start = lax.axis_index("grp") * col_width
    held = mix_lead(lax.all_to_all(grp_mixed, "row", split_axis=1, concat_axis=0, tiled=True))
    slice_width = held.shape[1]
    block_pos = lax.broadcasted_iota(jnp.int32, (n_row, slice_width), 0)
    inner_pos = lax.broadcasted_iota(jnp.int32, (n_row, slice_width), 1)
    held_ids = (
        (block_pos * n_grp + lax.axis_index("grp")) * rows_dev
        + lax.axis_index("row") * slice_width
        + inner_pos
    ).reshape(-1)
    found_pos = jnp.clip(jnp.searchsorted(sample_rows, held_ids), 0, num_samples - 1)
    is_sampled = jnp.take(sample_rows, found_pos) == held_ids
    held_flat = held.reshape(n_row * slice_width, n_cols)
    sketch_held = jnp.where(is_sampled[:, None], held_flat * norm_scale, 0.0).astype(jnp.bfloat16)
    shard_rows = lax.all_gather(sketch_held, "grp", axis=0, tiled=True)
    own_cols = lax.dynamic_slice_in_dim(shard_rows, col_start, col_width, 1)
    partial_value = lax.dot_general(
        shard_rows, own_cols, (((0,), (0,)), ((), ())), preferred_element_type=jnp.float32
    )
    gram_block = lax.psum_scatter(partial_value, "row", scatter_dimension=0, tiled=True)
    gathered = lax.all_gather(gram_block[None], ("row", "grp"), axis=0, tiled=True)
    gram_matrix = (
        gathered.reshape(n_row, n_grp, n_cols // n_row, col_width)
        .transpose(0, 2, 1, 3)
        .reshape(n_cols, n_cols)
    )
    lower_factor = jnp.linalg.cholesky(gram_matrix)
    row_width = n_cols // n_row
    return lax.dynamic_slice(
        lower_factor, (lax.axis_index("row") * row_width, col_start), (row_width, col_width)
    )


TA = (((0,), (0,)), ((), ()))
LEFT = (0, 0, 1, 0, 2, 1)
RIGHT = (0, 1, 0, 2, 0, 1)


def split(x):
    hi = x.astype(jnp.bfloat16)
    rest = x - hi.astype(f32)
    mid = rest.astype(jnp.bfloat16)
    return hi, mid, (rest - mid.astype(f32)).astype(jnp.bfloat16)


def mm6(a, b, ca, cb):
    lhs = jnp.concatenate([a[i] for i in LEFT], axis=ca)
    rhs = jnp.concatenate([b[i] for i in RIGHT], axis=cb)
    return lax.dot_general(lhs, rhs, (((ca,), (cb,)), ((), ())), preferred_element_type=f32)


def mm(a, b, dims=(((1,), (0,)), ((), ()))):
    return mm6(split(a), split(b), dims[0][0][0], dims[0][1][0])


def elim(X, sbase, ibase, n, zero=None):
    G=n//8
    xs=[X[8*g:8*g+8,:] for g in range(G)]
    rid=lax.broadcasted_iota(jnp.int32,(8,128),0)
    full=lambda v: jnp.broadcast_to(v,(8,128))
    out=[]
    for g in range(G):
        C=[[None]*G for _ in range(8)]
        for m in range(8):
            for h in range(g,G):
                l=sbase+8*g+m
                C[m][h]=full(xs[h][:,l:l+1])
        for m in range(8): C[m][g]=C[m][g]+zero
        o=jnp.zeros((8,128),f32)
        for j in range(0,8,2):
            a=full(C[j][g][j:j+1,:]); b=full(C[j][g][j+1:j+2,:]); c=full(C[j+1][g][j+1:j+2,:])
            r0=full(xs[g][j:j+1,:]); r1=full(xs[g][j+1:j+2,:])
            det=a*c-b*b
            inv=1.0/det
            ws=[]
            for m in range(j+2,8):
                q0=full(C[m][g][j:j+1,:]); q1=full(C[m][g][j+1:j+2,:])
                if j==0:
                    q0=q0; q1=q1
                ws.append((m,(c*q0-b*q1)*inv,(a*q1-b*q0)*inv))
            t1=a*r1-b*r0
            u0=(c*r0-b*r1)*inv; u1=t1*inv
            for m,w0,w1 in ws:
                for h in range(g,G):
                    C[m][h]=C[m][h]-C[j][h]*w0-C[j+1][h]*w1
            for h in range(g,G):
                if h>g or j<6:
                    xs[h]=xs[h]-C[j][h]*u0-C[j+1][h]*u1
            l0=r0*lax.rsqrt(a); l1=t1*lax.rsqrt(a*det)
            o=jnp.where(rid==j,l0,jnp.where(rid==j+1,l1,o))
        out.append(o)
    return jnp.concatenate(out,axis=0)

def factor128(D,zero):
    lane=lax.broadcasted_iota(jnp.int32,(64,128),1)
    row=lax.broadcasted_iota(jnp.int32,(64,128),0)
    z=jnp.zeros((64,128),f32)
    def equil(S,off,ioff):
        e=lane==row+off
        dg=jnp.where(e,S,0.0)
        dc=lax.rsqrt(jnp.sum(dg,axis=1,keepdims=True))
        dsum=jnp.sum(dg,axis=0,keepdims=True)
        half=(lane>=off)&(lane<off+64)
        drow=jnp.where(half[0:1],dsum,1.0)
        dr=lax.rsqrt(drow)
        X=jnp.where(half,S*dc*dr,jnp.where(lane==row+ioff,dc,0.0))
        back=jnp.where(half[0:1],drow*dr,1.0)
        return X,back
    Dt=D[:64,:]; Db=D[64:,:]
    X1,bk1=equil(Dt,0,64)
    F1=elim(X1,0,64,64,zero)*bk1
    U1=mm(F1,jnp.concatenate([z,Dt],axis=0))
    U12=jnp.where(lane>=64,U1,0.0)
    T=mm(U12,U12,TA)
    D2=Db-T[64:,:]
    X2,bk2=equil(D2,64,0)
    F2=elim(X2,64,0,64,zero)*bk2
    W1=jnp.where(lane>=64,F1,0.0)
    Q=mm(U12,F1,TA)
    V=mm(F2,jnp.concatenate([Q[64:,:],z],axis=0))
    W1s=pltpu.roll(F1,64,1); Vs=pltpu.roll(V,64,1)
    lo=lane<64
    Wtop=jnp.where(lo,W1s,0.0)
    W2s=pltpu.roll(F2,64,1)
    Wbot=jnp.where(lo,-Vs,W2s)
    Utop=jnp.where(lo,jnp.where(lane>=row,F1,0.0),U1)
    Ubot=jnp.where((~lo)&(lane-64>=row),F2,0.0)
    return jnp.concatenate([Utop,Ubot],axis=0),jnp.concatenate([Wtop,Wbot],axis=0)


def sketch_gram_kernel(n_dev, me_ref, x_ref, m_ref, keep_ref, send_ref, s_ref, fold):
    n = x_ref.shape[2]
    nb = n // TILE
    per = x_ref.shape[1]

    def mix(c, _):
        cols = pl.ds(pl.multiple_of(c * TILE, TILE), TILE)
        for sub in range(per // 8):
            v = [x_ref[b, 8 * sub : 8 * sub + 8, cols] for b in range(n_dev)]
            h = 1
            while h < n_dev:
                w = list(v)
                for b in range(n_dev):
                    if not b & h:
                        w[b] = v[b] + v[b | h]
                        w[b | h] = v[b] - v[b | h]
                v = w
                h *= 2
            for b in range(0, n_dev, 2):
                r = (sub * n_dev + b) * 8
                pair = jnp.concatenate([v[b], v[b + 1]], axis=0) * m_ref[r : r + 16, :]
                s_ref[r : r + 16, cols] = pair.astype(jnp.bfloat16)
        return 0

    lax.fori_loop(0, nb, mix, 0)
    for k in range(nb):
        part = lax.dot_general(
            s_ref[:, k * TILE : (k + 1) * TILE],
            s_ref[:, k * TILE :],
            TA,
            preferred_element_type=f32,
        )
        panel, off = (k, 0) if k < nb // 2 else (nb - 1 - k, k + 1)
        fold[panel * TILE : (panel + 1) * TILE, off * TILE : (off + nb - k) * TILE] = part
    half = n_dev // 2
    me = me_ref[0]
    h = keep_ref.shape[1]

    def put(j, _):
        keep_ref[j] = fold[pl.ds(pl.multiple_of((j ^ me) * h, 8), h), :]
        send_ref[j] = fold[pl.ds(pl.multiple_of(((j + half) ^ me) * h, 8), h), :]
        return 0

    lax.fori_loop(0, half, put, 0)


def factor_kernel(n, pos_ref, own_ref, recv_ref, out_ref, fold, u_ref, strip, zref, turn, w_ref, uh, um, ul):
    B = TILE
    nb = n // B
    parts = (uh, um, ul)
    half = own_ref.shape[0]
    h = own_ref.shape[1]
    me = pos_ref[0]

    def get(j, _):
        fold[pl.ds(pl.multiple_of((j ^ me) * h, 8), h), :] = own_ref[j]
        fold[pl.ds(pl.multiple_of(((j + half) ^ me) * h, 8), h), :] = recv_ref[j]
        return 0

    lax.fori_loop(0, half, get, 0)
    zref[...] = jnp.zeros((8, 128), f32)

    def update(k):
        right = slice(k * B, n)
        panel, off = (k, 0) if k < nb // 2 else (nb - 1 - k, k + 1)
        rows = fold[panel * B : (panel + 1) * B, off * B : (off + nb - k) * B]
        if k:
            cols = slice(k * B, (k + 1) * B)
            rows = rows - mm6([u[: k * B, cols] for u in parts], [u[: k * B, right] for u in parts], 0, 0)
        strip[:, right] = rows

    def solve(k):
        if k == nb - 1:
            return
        right = slice((k + 1) * B, n)
        done = mm6(split(w_ref[...]), split(strip[:, right]), 1, 0)
        u_ref[k * B : (k + 1) * B, right] = done
        for u, v in zip(parts, split(done)):
            u[k * B : (k + 1) * B, right] = v

    def body(k, _):
        for kk in range(nb):
            pl.when(k == kk)(functools.partial(update, kk))
        kc = pl.multiple_of(k * B, B)
        U, W = factor128(strip[:, pl.ds(kc, B)], zref[...])
        w_ref[...] = W
        u_ref[pl.ds(kc, B), pl.ds(kc, B)] = U
        for kk in range(nb):
            pl.when(k == kk)(functools.partial(solve, kk))
        return 0

    lax.fori_loop(0, nb, body, 0)
    row_width, col_width = out_ref.shape
    first_row = pos_ref[1] * row_width
    first_col = pos_ref[2] * col_width
    lane_tile = pl.multiple_of(first_row // B * B, B)
    inner = pl.multiple_of(first_row % B, 8)
    for c in range(col_width // B):
        block = u_ref[pl.ds(pl.multiple_of(first_col + c * B, B), B), pl.ds(lane_tile, B)]
        turn[...] = block.T
        i = first_row + lax.broadcasted_iota(jnp.int32, (row_width, B), 0)
        j = first_col + c * B + lax.broadcasted_iota(jnp.int32, (row_width, B), 1)
        out_ref[:, c * B : (c + 1) * B] = jnp.where(j <= i, turn[pl.ds(inner, row_width), :], 0.0)


def xor_send(value, mask, n_dev):
    return lax.ppermute(value, AXES, [(d, d ^ mask) for d in range(n_dev)])


def local_fast(panel_rows, sign_bits, sample_rows):
    rows_dev, n = panel_rows.shape
    n_row = lax.axis_size("row")
    n_grp = lax.axis_size("grp")
    n_dev = n_row * n_grp
    per = rows_dev // n_dev
    num_samples = sample_rows.shape[0]
    norm_scale = 1.0 / math.sqrt(rows_dev * n_dev * num_samples)
    row_i = lax.axis_index("row")
    grp_i = lax.axis_index("grp")
    lin = row_i * n_grp + grp_i

    flipped = panel_rows * (1 - 2 * sign_bits).astype(jnp.bfloat16)[:, None]
    local_mix = jnp.dot(hadamard(rows_dev, jnp.bfloat16), flipped, preferred_element_type=f32)
    mixed = lax.all_to_all(local_mix, AXES, split_axis=0, concat_axis=0, tiled=True)
    mixed = mixed.reshape(n_dev, per, n)

    r = lax.iota(jnp.int32, rows_dev)
    held_ids = (r // 8 % n_dev) * rows_dev + lin * per + r // (8 * n_dev) * 8 + r % 8
    is_sampled = jnp.any(held_ids[:, None] == sample_rows[None, :], axis=1)
    weight = jnp.where(is_sampled, norm_scale, 0.0).astype(f32)
    weight = jnp.broadcast_to(weight[:, None], (rows_dev, TILE))

    grp_bits = [1 << b for b in range(n_grp.bit_length() - 1)]
    row_bits = [n_grp << b for b in range(n_row.bit_length() - 1)]
    stages = [row_bits[:1], row_bits[1:2] + grp_bits, row_bits[2:]]
    order = [bit for stage in stages for bit in reversed(stage)]
    place = jnp.int32(0)
    for bit in order:
        place = place * 2 + (lin & bit) // bit

    def mask_of(stage, step):
        return sum(bit for pos, bit in enumerate(stage) if step >> pos & 1)

    nb = n // TILE
    fold_rows = nb // 2 * TILE
    fold_cols = (nb + 1) * TILE
    h = fold_rows // n_dev
    half = n_dev // 2
    piece = jax.ShapeDtypeStruct((half, h, fold_cols), f32)
    vmem = pl.BlockSpec(memory_space=pltpu.VMEM)
    smem = pl.BlockSpec(memory_space=pltpu.SMEM)
    keep, send = pl.pallas_call(
        functools.partial(sketch_gram_kernel, n_dev),
        out_shape=(piece, piece),
        in_specs=[smem, vmem, vmem],
        out_specs=(vmem, vmem),
        scratch_shapes=[pltpu.VMEM((rows_dev, n), jnp.bfloat16), pltpu.VMEM((fold_rows, fold_cols), f32)],
        compiler_params=pltpu.CompilerParams(vmem_limit_bytes=40 << 20),
        name="sketch_gram",
    )(place[None], mixed, weight)

    total = keep + xor_send(send, mask_of(stages[0], 1), n_dev)
    for stage in stages[1:]:
        ways = 1 << len(stage)
        if ways == 1:
            continue
        parts = total.reshape(ways, total.shape[0] // ways, h, fold_cols)
        got = [xor_send(parts[s], mask_of(stage, s), n_dev) for s in range(1, ways)]
        total = parts[0]
        for g in got:
            total = total + g
    for stage in reversed(stages[1:]):
        ways = 1 << len(stage)
        if ways == 1:
            continue
        got = [xor_send(total, mask_of(stage, s), n_dev) for s in range(1, ways)]
        total = jnp.concatenate([total] + got, axis=0)
    other = xor_send(total, mask_of(stages[0], 1), n_dev)

    row_width = n // n_row
    col_width = n // n_grp
    return pl.pallas_call(
        functools.partial(factor_kernel, n),
        out_shape=jax.ShapeDtypeStruct((row_width, col_width), f32),
        in_specs=[smem, vmem, vmem],
        out_specs=vmem,
        scratch_shapes=[
            pltpu.VMEM((fold_rows, fold_cols), f32),
            pltpu.VMEM((n, n), f32),
            pltpu.VMEM((TILE, n), f32),
            pltpu.VMEM((8, 128), f32),
            pltpu.VMEM((TILE, TILE), f32),
            pltpu.VMEM((TILE, TILE), f32),
        ]
        + [pltpu.VMEM((n, n), jnp.bfloat16)] * 3,
        compiler_params=pltpu.CompilerParams(vmem_limit_bytes=40 << 20),
        name="factor",
    )(jnp.stack([place, row_i, grp_i]), total, other)


def local(panel_rows, sign_bits, sample_rows):
    rows_dev, n = panel_rows.shape
    n_row = lax.axis_size("row")
    n_grp = lax.axis_size("grp")
    n_dev = n_row * n_grp
    fits = (
        n % (2 * TILE) == 0
        and n_dev & (n_dev - 1) == 0
        and 2 <= n_row
        and n_dev <= 64
        and rows_dev % (8 * n_dev) == 0
        and n // 2 % (8 * n_dev) == 0
        and TILE % (n // n_row) == 0
        and n // n_row % 8 == 0
        and n // n_grp % TILE == 0
    )
    return (local_fast if fits else local_plain)(panel_rows, sign_bits, sample_rows)


def solution(mesh):
    return jax.shard_map(
        local,
        mesh=mesh,
        in_specs=(P(("row", "grp"), None), P(("row", "grp")), P()),
        out_specs=P("row", "grp"),
        check_vma=False,
    )
```

```python
import functools
import math

import jax
import jax.numpy as jnp
from jax import lax
from jax.experimental import pallas as pl
from jax.experimental.pallas import tpu as pltpu
from jax.sharding import PartitionSpec as P

AXES = ("row", "grp")
TILE = 128
f32 = jnp.float32


def hadamard(table_size, dtype):
    row_ids = lax.broadcasted_iota(jnp.int32, (table_size, table_size), 0)
    col_ids = lax.broadcasted_iota(jnp.int32, (table_size, table_size), 1)
    shared = row_ids & col_ids
    parity = jnp.zeros((table_size, table_size), jnp.int32)
    for bit_pos in range(table_size.bit_length() - 1):
        parity = parity ^ shared >> bit_pos & 1
    return (1 - 2 * parity).astype(dtype)


def mix_lead(exchanged):
    lead_table = hadamard(exchanged.shape[0], jnp.float32)
    return jnp.einsum("ab,bic->aic", lead_table, exchanged, precision=lax.Precision.HIGHEST)


def mix_grp(exchanged):
    return lax.all_to_all(mix_lead(exchanged), "grp", split_axis=0, concat_axis=2, tiled=True)


def local_plain(panel_rows, sign_bits, sample_rows):
    rows_dev, n_cols = panel_rows.shape
    n_row = lax.axis_size("row")
    n_grp = lax.axis_size("grp")
    flipped = panel_rows * (1 - 2 * sign_bits).astype(jnp.bfloat16)[:, None]
    local_table = hadamard(rows_dev, jnp.bfloat16)
    local_mix = jnp.dot(local_table, flipped, preferred_element_type=jnp.float32)
    grp_mixed = mix_grp(
        lax.all_to_all(local_mix[None], "grp", split_axis=2, concat_axis=0, tiled=True)
    )
    num_samples = sample_rows.shape[0]
    total_rows = rows_dev * n_row * n_grp
    norm_scale = 1.0 / math.sqrt(total_rows * num_samples)
    col_width = n_cols // n_grp
    col_start = lax.axis_index("grp") * col_width
    held = mix_lead(lax.all_to_all(grp_mixed, "row", split_axis=1, concat_axis=0, tiled=True))
    slice_width = held.shape[1]
    block_pos = lax.broadcasted_iota(jnp.int32, (n_row, slice_width), 0)
    inner_pos = lax.broadcasted_iota(jnp.int32, (n_row, slice_width), 1)
    held_ids = (
        (block_pos * n_grp + lax.axis_index("grp")) * rows_dev
        + lax.axis_index("row") * slice_width
        + inner_pos
    ).reshape(-1)
    found_pos = jnp.clip(jnp.searchsorted(sample_rows, held_ids), 0, num_samples - 1)
    is_sampled = jnp.take(sample_rows, found_pos) == held_ids
    held_flat = held.reshape(n_row * slice_width, n_cols)
    sketch_held = jnp.where(is_sampled[:, None], held_flat * norm_scale, 0.0).astype(jnp.bfloat16)
    shard_rows = lax.all_gather(sketch_held, "grp", axis=0, tiled=True)
    own_cols = lax.dynamic_slice_in_dim(shard_rows, col_start, col_width, 1)
    partial_value = lax.dot_general(
        shard_rows, own_cols, (((0,), (0,)), ((), ())), preferred_element_type=jnp.float32
    )
    gram_block = lax.psum_scatter(partial_value, "row", scatter_dimension=0, tiled=True)
    gathered = lax.all_gather(gram_block[None], ("row", "grp"), axis=0, tiled=True)
    gram_matrix = (
        gathered.reshape(n_row, n_grp, n_cols // n_row, col_width)
        .transpose(0, 2, 1, 3)
        .reshape(n_cols, n_cols)
    )
    lower_factor = jnp.linalg.cholesky(gram_matrix)
    row_width = n_cols // n_row
    return lax.dynamic_slice(
        lower_factor, (lax.axis_index("row") * row_width, col_start), (row_width, col_width)
    )


TA = (((0,), (0,)), ((), ()))
LEFT = (0, 0, 1, 0, 2, 1)
RIGHT = (0, 1, 0, 2, 0, 1)


def split(x):
    hi = x.astype(jnp.bfloat16)
    rest = x - hi.astype(f32)
    mid = rest.astype(jnp.bfloat16)
    return hi, mid, (rest - mid.astype(f32)).astype(jnp.bfloat16)


def mm6(a, b, ca, cb):
    lhs = jnp.concatenate([a[i] for i in LEFT], axis=ca)
    rhs = jnp.concatenate([b[i] for i in RIGHT], axis=cb)
    return lax.dot_general(lhs, rhs, (((ca,), (cb,)), ((), ())), preferred_element_type=f32)


def eliminate(X, first, zero):
    G = X.shape[0] // 8
    xs = [X[8 * g : 8 * g + 8, :] for g in range(G)]
    rid = lax.broadcasted_iota(jnp.int32, (8, TILE), 0)

    def full(v):
        return jnp.broadcast_to(v, (8, TILE))

    def col(h, at):
        return full(xs[h][:, first + at : first + at + 1])

    out = []
    D = [col(0, m) + zero for m in range(8)]
    for g in range(G):
        C = D
        more = g + 1 < G
        near = [col(g + 1, 8 * g + m) for m in range(8)] if more else None
        D = [col(g + 1, 8 * g + 8 + m) for m in range(8)] if more else None
        far = {h: [col(h, 8 * g + m) for m in range(8)] for h in range(g + 2, G)}
        o = jnp.zeros((8, TILE), f32)
        for j in range(0, 8, 2):
            a = full(C[j][j : j + 1, :])
            b = full(C[j][j + 1 : j + 2, :])
            c = full(C[j + 1][j + 1 : j + 2, :])
            det = a * c - b * b
            inv = 1.0 / det
            ws = {}
            for m in range(j + 2, 8):
                q0 = full(C[m][j : j + 1, :])
                q1 = full(C[m][j + 1 : j + 2, :])
                t0 = c * q0 - b * q1
                t1 = a * q1 - b * q0
                ws[m] = t0 * inv, t1 * inv
                C[m] = C[m] - (C[j] * t0 + C[j + 1] * t1) * inv
            if more:
                n0 = c * near[j] - b * near[j + 1]
                n1 = a * near[j + 1] - b * near[j]
                if j == 6:
                    for m in range(8):
                        D[m] = D[m] - (near[j] * full(n0[m : m + 1, :]) + near[j + 1] * full(n1[m : m + 1, :])) * inv
                else:
                    v0 = n0 * inv
                    v1 = n1 * inv
                    for m in range(8):
                        D[m] = D[m] - near[j] * full(v0[m : m + 1, :]) - near[j + 1] * full(v1[m : m + 1, :])
            r0 = full(xs[g][j : j + 1, :])
            r1 = full(xs[g][j + 1 : j + 2, :])
            t1 = a * r1 - b * r0
            u0 = (c * r0 - b * r1) * inv
            u1 = t1 * inv
            if j < 6:
                xs[g] = xs[g] - C[j] * u0 - C[j + 1] * u1
            if more:
                xs[g + 1] = xs[g + 1] - near[j] * u0 - near[j + 1] * u1
                for m, (w0, w1) in ws.items():
                    near[m] = near[m] - near[j] * w0 - near[j + 1] * w1
            for h, cols in far.items():
                xs[h] = xs[h] - cols[j] * u0 - cols[j + 1] * u1
                for m, (w0, w1) in ws.items():
                    cols[m] = cols[m] - cols[j] * w0 - cols[j + 1] * w1
            l0 = r0 * lax.rsqrt(a)
            l1 = t1 * lax.rsqrt(a * det)
            o = jnp.where(rid == j, l0, jnp.where(rid == j + 1, l1, o))
        out.append(o)
    return jnp.concatenate(out, axis=0)


def scaled(S, off, other):
    lane = lax.broadcasted_iota(jnp.int32, S.shape, 1)
    row = lax.broadcasted_iota(jnp.int32, S.shape, 0)
    diag = jnp.where(lane == row + off, S, 0.0)
    down = lax.rsqrt(jnp.sum(diag, axis=1, keepdims=True))
    half = (lane >= off) & (lane < off + S.shape[0])
    across = jnp.where(half[0:1], jnp.sum(diag, axis=0, keepdims=True), 1.0)
    root = lax.rsqrt(across)
    X = jnp.where(half, S * down * root, jnp.where(lane == row + other, down, 0.0))
    return X, jnp.where(half[0:1], across * root, 1.0)


def sketch_gram_kernel(n_dev, me_ref, x_ref, m_ref, keep_ref, send_ref, s_ref, fold):
    n = x_ref.shape[2]
    nb = n // TILE
    per = x_ref.shape[1]

    def mix(c, _):
        cols = pl.ds(pl.multiple_of(c * TILE, TILE), TILE)
        for sub in range(per // 8):
            v = [x_ref[b, 8 * sub : 8 * sub + 8, cols] for b in range(n_dev)]
            h = 1
            while h < n_dev:
                w = list(v)
                for b in range(n_dev):
                    if not b & h:
                        w[b] = v[b] + v[b | h]
                        w[b | h] = v[b] - v[b | h]
                v = w
                h *= 2
            for b in range(0, n_dev, 2):
                r = (sub * n_dev + b) * 8
                pair = jnp.concatenate([v[b], v[b + 1]], axis=0) * m_ref[r : r + 16, :]
                s_ref[r : r + 16, cols] = pair.astype(jnp.bfloat16)
        return 0

    lax.fori_loop(0, nb, mix, 0)
    for k in range(nb):
        part = lax.dot_general(
            s_ref[:, k * TILE : (k + 1) * TILE],
            s_ref[:, k * TILE :],
            TA,
            preferred_element_type=f32,
        )
        panel, off = (k, 0) if k < nb // 2 else (nb - 1 - k, k + 1)
        fold[panel * TILE : (panel + 1) * TILE, off * TILE : (off + nb - k) * TILE] = part
    half = n_dev // 2
    me = me_ref[0]
    h = keep_ref.shape[1]

    def put(j, _):
        keep_ref[j] = fold[pl.ds(pl.multiple_of((j ^ me) * h, 8), h), :]
        send_ref[j] = fold[pl.ds(pl.multiple_of(((j + half) ^ me) * h, 8), h), :]
        return 0

    lax.fori_loop(0, half, put, 0)


def factor_kernel(n, pos_ref, own_ref, recv_ref, out_ref, fold, zref, turn, uh, um, ul):
    B = TILE
    H = B // 2
    nb = n // B
    parts = (uh, um, ul)
    half = own_ref.shape[0]
    h = own_ref.shape[1]
    me = pos_ref[0]

    def get(j, _):
        fold[pl.ds(pl.multiple_of((j ^ me) * h, 8), h), :] = own_ref[j]
        fold[pl.ds(pl.multiple_of(((j + half) ^ me) * h, 8), h), :] = recv_ref[j]
        return 0

    lax.fori_loop(0, half, get, 0)
    zref[...] = jnp.zeros((8, B), f32)
    lane = lax.broadcasted_iota(jnp.int32, (H, B), 1)
    row = lax.broadcasted_iota(jnp.int32, (H, B), 0)
    low = lane < H

    def gram(k, j0, j1):
        panel, off = (k, -k) if k < nb // 2 else (nb - 1 - k, 1)
        return fold[panel * B : (panel + 1) * B, (j0 + off) * B : (j1 + off) * B]

    def store(r, cols, value):
        value = split(value)
        for u, v in zip(parts, value):
            u[r : r + H, cols] = v
        return value

    def under(value, top):
        zero = jnp.zeros(value.shape, jnp.bfloat16)
        return [jnp.concatenate([zero, v] if top else [v, zero], axis=0) for v in split(value)]

    D = gram(0, 0, 1)
    for k in range(nb):
        r = k * B
        here = slice(r, r + B)
        rest = slice(r + B, n)
        then = slice(r + B, r + 2 * B)
        tail = k < nb - 1
        X1, back1 = scaled(D[:H], 0, H)
        if tail:
            R = gram(k, k + 1, nb)
            E = gram(k + 1, k + 1, k + 2)
            if k:
                R = R - mm6([u[:r, here] for u in parts], [u[:r, rest] for u in parts], 0, 0)
                E = E - mm6([u[:r, then] for u in parts], [u[:r, then] for u in parts], 0, 0)
        F1 = eliminate(X1, 0, zref[...]) * back1
        f1 = split(F1)
        U1 = mm6(f1, under(D[:H], True), 1, 0)
        u12 = split(jnp.where(low, 0.0, U1))
        D2 = D[H:] - mm6(u12, u12, 0, 0)[H:]
        X2, back2 = scaled(D2, H, 0)
        store(r, here, jnp.where(low, jnp.where(lane >= row, F1, 0.0), U1))
        if tail:
            P1 = mm6(f1, under(R[:H], True), 1, 0)
            p1 = store(r, rest, P1)
            R2 = R[H:] - mm6(u12, p1, 0, 0)[H:]
            p1 = [v[:, :B] for v in p1]
            E = E - mm6(p1, p1, 0, 0)
        F2 = eliminate(X2, H, zref[...]) * back2
        store(r + H, here, jnp.where(low | (lane - H < row), 0.0, F2))
        if tail:
            P2 = mm6(split(F2), under(R2, False), 1, 0)
            p2 = [v[:, :B] for v in store(r + H, rest, P2)]
            D = E - mm6(p2, p2, 0, 0)
    row_width, col_width = out_ref.shape
    first_row = pos_ref[1] * row_width
    first_col = pos_ref[2] * col_width
    lane_tile = pl.multiple_of(first_row // B * B, B)
    inner = pl.multiple_of(first_row % B, 8)
    for c in range(col_width // B):
        where = (pl.ds(pl.multiple_of(first_col + c * B, B), B), pl.ds(lane_tile, B))
        hi, mid, tiny = (u[where].astype(f32) for u in parts)
        turn[...] = ((tiny + mid) + hi).T
        i = first_row + lax.broadcasted_iota(jnp.int32, (row_width, B), 0)
        j = first_col + c * B + lax.broadcasted_iota(jnp.int32, (row_width, B), 1)
        out_ref[:, c * B : (c + 1) * B] = jnp.where(j <= i, turn[pl.ds(inner, row_width), :], 0.0)


def xor_send(value, mask, n_dev):
    return lax.ppermute(value, AXES, [(d, d ^ mask) for d in range(n_dev)])


def local_fast(panel_rows, sign_bits, sample_rows):
    rows_dev, n = panel_rows.shape
    n_row = lax.axis_size("row")
    n_grp = lax.axis_size("grp")
    n_dev = n_row * n_grp
    per = rows_dev // n_dev
    num_samples = sample_rows.shape[0]
    norm_scale = 1.0 / math.sqrt(rows_dev * n_dev * num_samples)
    row_i = lax.axis_index("row")
    grp_i = lax.axis_index("grp")
    lin = row_i * n_grp + grp_i

    flipped = panel_rows * (1 - 2 * sign_bits).astype(jnp.bfloat16)[:, None]
    local_mix = jnp.dot(hadamard(rows_dev, jnp.bfloat16), flipped, preferred_element_type=f32)
    mixed = lax.all_to_all(local_mix, AXES, split_axis=0, concat_axis=0, tiled=True)
    mixed = mixed.reshape(n_dev, per, n)

    r = lax.iota(jnp.int32, rows_dev)
    held_ids = (r // 8 % n_dev) * rows_dev + lin * per + r // (8 * n_dev) * 8 + r % 8
    is_sampled = jnp.any(held_ids[:, None] == sample_rows[None, :], axis=1)
    weight = jnp.where(is_sampled, norm_scale, 0.0).astype(f32)
    weight = jnp.broadcast_to(weight[:, None], (rows_dev, TILE))

    grp_bits = [1 << b for b in range(n_grp.bit_length() - 1)]
    row_bits = [n_grp << b for b in range(n_row.bit_length() - 1)]
    stages = [row_bits[:1], row_bits[1:2] + grp_bits, row_bits[2:]]
    order = [bit for stage in stages for bit in reversed(stage)]
    place = jnp.int32(0)
    for bit in order:
        place = place * 2 + (lin & bit) // bit

    def mask_of(stage, step):
        return sum(bit for pos, bit in enumerate(stage) if step >> pos & 1)

    nb = n // TILE
    fold_rows = nb // 2 * TILE
    fold_cols = (nb + 1) * TILE
    h = fold_rows // n_dev
    half = n_dev // 2
    piece = jax.ShapeDtypeStruct((half, h, fold_cols), f32)
    vmem = pl.BlockSpec(memory_space=pltpu.VMEM)
    smem = pl.BlockSpec(memory_space=pltpu.SMEM)
    keep, send = pl.pallas_call(
        functools.partial(sketch_gram_kernel, n_dev),
        out_shape=(piece, piece),
        in_specs=[smem, vmem, vmem],
        out_specs=(vmem, vmem),
        scratch_shapes=[pltpu.VMEM((rows_dev, n), jnp.bfloat16), pltpu.VMEM((fold_rows, fold_cols), f32)],
        compiler_params=pltpu.CompilerParams(vmem_limit_bytes=40 << 20),
        name="sketch_gram",
    )(place[None], mixed, weight)

    total = keep + xor_send(send, mask_of(stages[0], 1), n_dev)
    for stage in stages[1:]:
        ways = 1 << len(stage)
        if ways == 1:
            continue
        parts = total.reshape(ways, total.shape[0] // ways, h, fold_cols)
        got = [xor_send(parts[s], mask_of(stage, s), n_dev) for s in range(1, ways)]
        total = parts[0]
        for g in got:
            total = total + g
    for stage in reversed(stages[1:]):
        ways = 1 << len(stage)
        if ways == 1:
            continue
        got = [xor_send(total, mask_of(stage, s), n_dev) for s in range(1, ways)]
        total = jnp.concatenate([total] + got, axis=0)
    other = xor_send(total, mask_of(stages[0], 1), n_dev)

    row_width = n // n_row
    col_width = n // n_grp
    return pl.pallas_call(
        functools.partial(factor_kernel, n),
        out_shape=jax.ShapeDtypeStruct((row_width, col_width), f32),
        in_specs=[smem, vmem, vmem],
        out_specs=vmem,
        scratch_shapes=[
            pltpu.VMEM((fold_rows, fold_cols), f32),
            pltpu.VMEM((8, TILE), f32),
            pltpu.VMEM((TILE, TILE), f32),
        ]
        + [pltpu.VMEM((n, n), jnp.bfloat16)] * 3,
        compiler_params=pltpu.CompilerParams(vmem_limit_bytes=40 << 20),
        name="factor",
    )(jnp.stack([place, row_i, grp_i]), total, other)


def local(panel_rows, sign_bits, sample_rows):
    rows_dev, n = panel_rows.shape
    n_row = lax.axis_size("row")
    n_grp = lax.axis_size("grp")
    n_dev = n_row * n_grp
    fits = (
        n % (2 * TILE) == 0
        and n_dev & (n_dev - 1) == 0
        and 2 <= n_row
        and n_dev <= 64
        and rows_dev % (8 * n_dev) == 0
        and n // 2 % (8 * n_dev) == 0
        and TILE % (n // n_row) == 0
        and n // n_row % 8 == 0
        and n // n_grp % TILE == 0
    )
    return (local_fast if fits else local_plain)(panel_rows, sign_bits, sample_rows)


def solution(mesh):
    return jax.shard_map(
        local,
        mesh=mesh,
        in_specs=(P(("row", "grp"), None), P(("row", "grp")), P()),
        out_specs=P("row", "grp"),
        check_vma=False,
    )
```

```python
import functools
import math

import jax
import jax.numpy as jnp
from jax import lax
from jax.experimental import pallas as pl
from jax.experimental.pallas import tpu as pltpu
from jax.sharding import PartitionSpec as P

AXES = ("row", "grp")
TILE = 128
f32 = jnp.float32


def hadamard(table_size, dtype):
    row_ids = lax.broadcasted_iota(jnp.int32, (table_size, table_size), 0)
    col_ids = lax.broadcasted_iota(jnp.int32, (table_size, table_size), 1)
    shared = row_ids & col_ids
    parity = jnp.zeros((table_size, table_size), jnp.int32)
    for bit_pos in range(table_size.bit_length() - 1):
        parity = parity ^ shared >> bit_pos & 1
    return (1 - 2 * parity).astype(dtype)


def mix_lead(exchanged):
    lead_table = hadamard(exchanged.shape[0], jnp.float32)
    return jnp.einsum("ab,bic->aic", lead_table, exchanged, precision=lax.Precision.HIGHEST)


def mix_grp(exchanged):
    return lax.all_to_all(mix_lead(exchanged), "grp", split_axis=0, concat_axis=2, tiled=True)


def local_plain(panel_rows, sign_bits, sample_rows):
    rows_dev, n_cols = panel_rows.shape
    n_row = lax.axis_size("row")
    n_grp = lax.axis_size("grp")
    flipped = panel_rows * (1 - 2 * sign_bits).astype(jnp.bfloat16)[:, None]
    local_table = hadamard(rows_dev, jnp.bfloat16)
    local_mix = jnp.dot(local_table, flipped, preferred_element_type=jnp.float32)
    grp_mixed = mix_grp(
        lax.all_to_all(local_mix[None], "grp", split_axis=2, concat_axis=0, tiled=True)
    )
    num_samples = sample_rows.shape[0]
    total_rows = rows_dev * n_row * n_grp
    norm_scale = 1.0 / math.sqrt(total_rows * num_samples)
    col_width = n_cols // n_grp
    col_start = lax.axis_index("grp") * col_width
    held = mix_lead(lax.all_to_all(grp_mixed, "row", split_axis=1, concat_axis=0, tiled=True))
    slice_width = held.shape[1]
    block_pos = lax.broadcasted_iota(jnp.int32, (n_row, slice_width), 0)
    inner_pos = lax.broadcasted_iota(jnp.int32, (n_row, slice_width), 1)
    held_ids = (
        (block_pos * n_grp + lax.axis_index("grp")) * rows_dev
        + lax.axis_index("row") * slice_width
        + inner_pos
    ).reshape(-1)
    found_pos = jnp.clip(jnp.searchsorted(sample_rows, held_ids), 0, num_samples - 1)
    is_sampled = jnp.take(sample_rows, found_pos) == held_ids
    held_flat = held.reshape(n_row * slice_width, n_cols)
    sketch_held = jnp.where(is_sampled[:, None], held_flat * norm_scale, 0.0).astype(jnp.bfloat16)
    shard_rows = lax.all_gather(sketch_held, "grp", axis=0, tiled=True)
    own_cols = lax.dynamic_slice_in_dim(shard_rows, col_start, col_width, 1)
    partial_value = lax.dot_general(
        shard_rows, own_cols, (((0,), (0,)), ((), ())), preferred_element_type=jnp.float32
    )
    gram_block = lax.psum_scatter(partial_value, "row", scatter_dimension=0, tiled=True)
    gathered = lax.all_gather(gram_block[None], ("row", "grp"), axis=0, tiled=True)
    gram_matrix = (
        gathered.reshape(n_row, n_grp, n_cols // n_row, col_width)
        .transpose(0, 2, 1, 3)
        .reshape(n_cols, n_cols)
    )
    lower_factor = jnp.linalg.cholesky(gram_matrix)
    row_width = n_cols // n_row
    return lax.dynamic_slice(
        lower_factor, (lax.axis_index("row") * row_width, col_start), (row_width, col_width)
    )


TA = (((0,), (0,)), ((), ()))
LEFT = (0, 0, 1, 0, 2, 1)
RIGHT = (0, 1, 0, 2, 0, 1)


def split(x):
    hi = x.astype(jnp.bfloat16)
    rest = x - hi.astype(f32)
    mid = rest.astype(jnp.bfloat16)
    return hi, mid, (rest - mid.astype(f32)).astype(jnp.bfloat16)


def mm6(a, b, ca, cb):
    lhs = jnp.concatenate([a[i] for i in LEFT], axis=ca)
    rhs = jnp.concatenate([b[i] for i in RIGHT], axis=cb)
    return lax.dot_general(lhs, rhs, (((ca,), (cb,)), ((), ())), preferred_element_type=f32)


def eliminate(X, first, zero):
    G = X.shape[0] // 8
    xs = [X[8 * g : 8 * g + 8, :] for g in range(G)]
    rid = lax.broadcasted_iota(jnp.int32, (8, TILE), 0)

    def full(v):
        return jnp.broadcast_to(v, (8, TILE))

    def col(h, at):
        return full(xs[h][:, first + at : first + at + 1])

    out = []
    D = [col(0, m) + zero for m in range(8)]
    for g in range(G):
        C = D
        more = g + 1 < G
        near = [col(g + 1, 8 * g + m) for m in range(8)] if more else None
        D = [col(g + 1, 8 * g + 8 + m) for m in range(8)] if more else None
        far = {h: [col(h, 8 * g + m) for m in range(8)] for h in range(g + 2, G)}
        o = jnp.zeros((8, TILE), f32)
        for j in range(0, 8, 2):
            a = full(C[j][j : j + 1, :])
            b = full(C[j][j + 1 : j + 2, :])
            c = full(C[j + 1][j + 1 : j + 2, :])
            det = a * c - b * b
            inv = 1.0 / det
            ws = {}
            for m in range(j + 2, 8):
                q0 = full(C[m][j : j + 1, :])
                q1 = full(C[m][j + 1 : j + 2, :])
                t0 = c * q0 - b * q1
                t1 = a * q1 - b * q0
                ws[m] = t0 * inv, t1 * inv
                C[m] = C[m] - (C[j] * t0 + C[j + 1] * t1) * inv
            if more:
                n0 = c * near[j] - b * near[j + 1]
                n1 = a * near[j + 1] - b * near[j]
                if j == 6:
                    for m in range(8):
                        D[m] = D[m] - (near[j] * full(n0[m : m + 1, :]) + near[j + 1] * full(n1[m : m + 1, :])) * inv
                else:
                    v0 = n0 * inv
                    v1 = n1 * inv
                    for m in range(8):
                        D[m] = D[m] - near[j] * full(v0[m : m + 1, :]) - near[j + 1] * full(v1[m : m + 1, :])
            r0 = full(xs[g][j : j + 1, :])
            r1 = full(xs[g][j + 1 : j + 2, :])
            t1 = a * r1 - b * r0
            u0 = (c * r0 - b * r1) * inv
            u1 = t1 * inv
            if j < 6:
                xs[g] = xs[g] - C[j] * u0 - C[j + 1] * u1
            if more:
                xs[g + 1] = xs[g + 1] - near[j] * u0 - near[j + 1] * u1
                for m, (w0, w1) in ws.items():
                    near[m] = near[m] - near[j] * w0 - near[j + 1] * w1
            for h, cols in far.items():
                xs[h] = xs[h] - cols[j] * u0 - cols[j + 1] * u1
                for m, (w0, w1) in ws.items():
                    cols[m] = cols[m] - cols[j] * w0 - cols[j + 1] * w1
            l0 = r0 * lax.rsqrt(a)
            l1 = t1 * lax.rsqrt(a * det)
            o = jnp.where(rid == j, l0, jnp.where(rid == j + 1, l1, o))
        out.append(o)
    return jnp.concatenate(out, axis=0)


def scaled(S, off, other):
    lane = lax.broadcasted_iota(jnp.int32, S.shape, 1)
    row = lax.broadcasted_iota(jnp.int32, S.shape, 0)
    diag = jnp.where(lane == row + off, S, 0.0)
    down = lax.rsqrt(jnp.sum(diag, axis=1, keepdims=True))
    half = (lane >= off) & (lane < off + S.shape[0])
    across = jnp.where(half[0:1], jnp.sum(diag, axis=0, keepdims=True), 1.0)
    root = lax.rsqrt(across)
    X = jnp.where(half, S * down * root, jnp.where(lane == row + other, down, 0.0))
    return X, jnp.where(half[0:1], across * root, 1.0)


def local_kernel(sign_ref, panel_ref, out_ref, signed):
    blocks = panel_ref.shape[0] // TILE

    @pl.when(pl.program_id(0) == 0)
    def _():
        table = hadamard(TILE, f32)
        for b in range(blocks):
            sign = 1 - 2 * sign_ref[:, b * TILE : (b + 1) * TILE]
            signed[b] = (table * sign.astype(f32)).astype(jnp.bfloat16)

    v = [
        jnp.dot(signed[b], panel_ref[b * TILE : (b + 1) * TILE, :], preferred_element_type=f32) for b in range(blocks)
    ]
    h = 1
    while h < blocks:
        w = list(v)
        for b in range(blocks):
            if not b & h:
                w[b] = v[b] + v[b | h]
                w[b | h] = v[b] - v[b | h]
        v = w
        h *= 2
    for b in range(blocks):
        out_ref[b * TILE : (b + 1) * TILE, :] = v[b]


def cells_of(nb):
    cells = []
    for k in range(nb):
        cells.append(("top", k))
        cells += [("full", k, j, i) for j in range(k + 1, nb) for i in range(2)]
        if k % 2 == 0:
            cells.append(("low", k // 2))
    return cells


def head_tiles(nb, panels, deep):
    cells = cells_of(nb)
    need = [c for c in cells if c[1] < panels and c[0] != "low" or c[0] == "low" and 2 * c[1] < panels]
    return -(-(1 + max(cells.index(c) for c in need)) // deep)


def slot(nb, deep, cell):
    at = cells_of(nb).index(cell)
    half = TILE // 2
    return slice(at % deep * half, (at % deep + 1) * half), slice(at // deep * TILE, (at // deep + 1) * TILE)


def sketch_gram_kernel(n_dev, me_ref, x_ref, m_ref, keep_ref, send_ref, s_ref, pack):
    n = x_ref.shape[2]
    nb = n // TILE
    per = x_ref.shape[1]

    def mix(c, _):
        cols = pl.ds(pl.multiple_of(c * TILE, TILE), TILE)
        for sub in range(per // 8):
            v = [x_ref[b, 8 * sub : 8 * sub + 8, cols] for b in range(n_dev)]
            h = 1
            while h < n_dev:
                w = list(v)
                for b in range(n_dev):
                    if not b & h:
                        w[b] = v[b] + v[b | h]
                        w[b | h] = v[b] - v[b | h]
                v = w
                h *= 2
            for b in range(0, n_dev, 2):
                r = (sub * n_dev + b) * 8
                pair = jnp.concatenate([v[b], v[b + 1]], axis=0) * m_ref[r : r + 16, :]
                s_ref[r : r + 16, cols] = pair.astype(jnp.bfloat16)
        return 0

    lax.fori_loop(0, nb, mix, 0)
    H = TILE // 2
    deep = pack.shape[0] // H
    lane = lax.broadcasted_iota(jnp.int32, (H, TILE), 1)
    even = None
    for k in range(nb):
        part = lax.dot_general(
            s_ref[:, k * TILE : (k + 1) * TILE],
            s_ref[:, k * TILE :],
            TA,
            preferred_element_type=f32,
        )
        pack[slot(nb, deep, ("top", k))] = part[:H, :TILE]
        for j in range(k + 1, nb):
            for i in range(2):
                cols = slice((j - k) * TILE, (j - k + 1) * TILE)
                pack[slot(nb, deep, ("full", k, j, i))] = part[i * H : (i + 1) * H, cols]
        if k % 2 == 0:
            even = part[H:, :TILE]
        else:
            odd = pltpu.roll(part[H:, :TILE], H, 1)
            pack[slot(nb, deep, ("low", k // 2))] = jnp.where(lane < H, odd, even)
    half = n_dev // 2
    me = me_ref[0]
    h = keep_ref.shape[1]

    def put(j, _):
        keep_ref[j] = pack[pl.ds(pl.multiple_of((j ^ me) * h, 8), h), :]
        send_ref[j] = pack[pl.ds(pl.multiple_of(((j + half) ^ me) * h, 8), h), :]
        return 0

    lax.fori_loop(0, half, put, 0)


def factor_kernel(n, p0, p1, head, pos_ref, own_ref, recv_ref, *refs):
    refs = list(refs)
    last = p1 == n // TILE
    old = [refs.pop(0) for _ in range(3)] if p0 else None
    kept = refs.pop(0) if p0 else None
    if last:
        out_ref = refs.pop(0)
        parts = refs[-3:]
    else:
        parts = [refs.pop(0) for _ in range(3)]
        keep_ref = refs.pop(0)
    pack, zref, turn = refs[:3]
    B = TILE
    H = B // 2
    nb = n // B
    half = own_ref.shape[0]
    h = own_ref.shape[1]
    me = pos_ref[0]

    def get(j, _):
        pack[pl.ds(pl.multiple_of((j ^ me) * h, 8), h), :] = own_ref[j]
        pack[pl.ds(pl.multiple_of(((j + half) ^ me) * h, 8), h), :] = recv_ref[j]
        return 0

    lax.fori_loop(0, half, get, 0)
    zref[...] = jnp.zeros((8, B), f32)
    lane = lax.broadcasted_iota(jnp.int32, (H, B), 1)
    row = lax.broadcasted_iota(jnp.int32, (H, B), 0)
    low = lane < H

    deep = pack.shape[0] // H

    def cell(*name):
        rows, lanes = slot(nb, deep, name)
        if p0 and lanes.start < head * B:
            return kept[rows, lanes.start - (head - 1) * B : lanes.stop - (head - 1) * B]
        base = head * B if p0 else 0
        return pack[rows, lanes.start - base : lanes.stop - base]

    def diagonal(k):
        low_part = cell("low", k // 2)
        return jnp.concatenate([cell("top", k), pltpu.roll(low_part, H, 1) if k % 2 else low_part], axis=0)

    def beside(k):
        rows = [jnp.concatenate([cell("full", k, j, i) for j in range(k + 1, nb)], axis=1) for i in range(2)]
        return jnp.concatenate(rows, axis=0)

    def above(k, cols):
        new = [u[: (k - p0) * B, cols] for u in parts]
        if not p0:
            return new
        if k == p0:
            return [u[:, cols] for u in old]
        return [jnp.concatenate([o[:, cols], u], axis=0) for o, u in zip(old, new)]

    def store(r, cols, value):
        value = split(value)
        for u, v in zip(parts, value):
            u[r - p0 * B : r - p0 * B + H, cols] = v
        return value

    def under(value, top):
        zero = jnp.zeros(value.shape, jnp.bfloat16)
        return [jnp.concatenate([zero, v] if top else [v, zero], axis=0) for v in split(value)]

    D = diagonal(p0)
    if p0:
        left = above(p0, slice(p0 * B, (p0 + 1) * B))
        D = D - mm6(left, left, 0, 0)
    for k in range(p0, p1):
        r = k * B
        here = slice(r, r + B)
        rest = slice(r + B, n)
        then = slice(r + B, r + 2 * B)
        tail = k < nb - 1
        X1, back1 = scaled(D[:H], 0, H)
        if tail:
            R = beside(k)
            if k:
                R = R - mm6(above(k, here), above(k, rest), 0, 0)
            if k < p1 - 1:
                E = diagonal(k + 1)
                if k:
                    left = above(k, then)
                    E = E - mm6(left, left, 0, 0)
        F1 = eliminate(X1, 0, zref[...]) * back1
        f1 = split(F1)
        U1 = mm6(f1, under(D[:H], True), 1, 0)
        u12 = split(jnp.where(low, 0.0, U1))
        D2 = D[H:] - mm6(u12, u12, 0, 0)[H:]
        X2, back2 = scaled(D2, H, 0)
        store(r, here, jnp.where(low, jnp.where(lane >= row, F1, 0.0), U1))
        if tail:
            P1 = mm6(f1, under(R[:H], True), 1, 0)
            first = store(r, rest, P1)
            R2 = R[H:] - mm6(u12, first, 0, 0)[H:]
            if k < p1 - 1:
                first = [v[:, :B] for v in first]
                E = E - mm6(first, first, 0, 0)
        F2 = eliminate(X2, H, zref[...]) * back2
        store(r + H, here, jnp.where(low | (lane - H < row), 0.0, F2))
        if tail:
            P2 = mm6(split(F2), under(R2, False), 1, 0)
            second = [v[:, :B] for v in store(r + H, rest, P2)]
            if k < p1 - 1:
                D = E - mm6(second, second, 0, 0)
    if not last:
        keep_ref[...] = pack[:, (head - 1) * B :]
        return
    row_width, col_width = out_ref.shape
    first_row = pos_ref[1] * row_width
    first_col = pos_ref[2] * col_width
    lane_tile = pl.multiple_of(first_row // B * B, B)
    inner = pl.multiple_of(first_row % B, 8)
    for c in range(col_width // B):
        rb = first_col // B + c

        def take(src, block):
            where = (pl.ds(pl.multiple_of(block * B, B), B), pl.ds(lane_tile, B))
            hi, mid, tiny = (u[where].astype(f32) for u in src)
            turn[...] = ((tiny + mid) + hi).T

        if p0:
            pl.when(rb < p0)(lambda: take(old, jnp.minimum(rb, p0 - 1)))
        pl.when(rb >= p0)(lambda: take(parts, jnp.clip(rb - p0, 0, nb - p0 - 1)))
        i = first_row + lax.broadcasted_iota(jnp.int32, (row_width, B), 0)
        j = first_col + c * B + lax.broadcasted_iota(jnp.int32, (row_width, B), 1)
        out_ref[:, c * B : (c + 1) * B] = jnp.where(j <= i, turn[pl.ds(inner, row_width), :], 0.0)


def xor_send(value, mask, n_dev):
    return lax.ppermute(value, AXES, [(d, d ^ mask) for d in range(n_dev)])


def local_fast(panel_rows, sign_bits, sample_rows):
    rows_dev, n = panel_rows.shape
    n_row = lax.axis_size("row")
    n_grp = lax.axis_size("grp")
    n_dev = n_row * n_grp
    per = rows_dev // n_dev
    num_samples = sample_rows.shape[0]
    norm_scale = 1.0 / math.sqrt(rows_dev * n_dev * num_samples)
    row_i = lax.axis_index("row")
    grp_i = lax.axis_index("grp")
    lin = row_i * n_grp + grp_i

    vmem = pl.BlockSpec(memory_space=pltpu.VMEM)
    smem = pl.BlockSpec(memory_space=pltpu.SMEM)
    width = 2 * TILE
    local_mix = pl.pallas_call(
        local_kernel,
        grid=(n // width,),
        out_shape=jax.ShapeDtypeStruct((rows_dev, n), f32),
        in_specs=[
            pl.BlockSpec((1, rows_dev), lambda c: (0, 0)),
            pl.BlockSpec((rows_dev, width), lambda c: (0, c)),
        ],
        out_specs=pl.BlockSpec((rows_dev, width), lambda c: (0, c)),
        scratch_shapes=[pltpu.VMEM((rows_dev // TILE, TILE, TILE), jnp.bfloat16)],
        compiler_params=pltpu.CompilerParams(vmem_limit_bytes=60 << 20),
        name="local_mix",
    )(sign_bits[None], panel_rows)
    mixed = lax.all_to_all(local_mix, AXES, split_axis=0, concat_axis=0, tiled=True)
    mixed = mixed.reshape(n_dev, per, n)

    r = lax.iota(jnp.int32, rows_dev)
    held_ids = (r // 8 % n_dev) * rows_dev + lin * per + r // (8 * n_dev) * 8 + r % 8
    is_sampled = jnp.any(held_ids[:, None] == sample_rows[None, :], axis=1)
    weight = jnp.where(is_sampled, norm_scale, 0.0).astype(f32)
    weight = jnp.broadcast_to(weight[:, None], (rows_dev, TILE))

    grp_bits = [1 << b for b in range(n_grp.bit_length() - 1)]
    row_bits = [n_grp << b for b in range(n_row.bit_length() - 1)]
    stages = [row_bits[:1], row_bits[1:2] + grp_bits, row_bits[2:]]
    order = [bit for stage in stages for bit in reversed(stage)]
    place = jnp.int32(0)
    for bit in order:
        place = place * 2 + (lin & bit) // bit

    def mask_of(stage, step):
        return sum(bit for pos, bit in enumerate(stage) if step >> pos & 1)

    nb = n // TILE
    rows = 8 * n_dev
    deep = rows // (TILE // 2)
    lanes = -(-len(cells_of(nb)) // deep) * TILE
    half = n_dev // 2
    piece = jax.ShapeDtypeStruct((half, 8, lanes), f32)
    keep, send = pl.pallas_call(
        functools.partial(sketch_gram_kernel, n_dev),
        out_shape=(piece, piece),
        in_specs=[smem, vmem, vmem],
        out_specs=(vmem, vmem),
        scratch_shapes=[pltpu.VMEM((rows_dev, n), jnp.bfloat16), pltpu.VMEM((rows, lanes), f32)],
        compiler_params=pltpu.CompilerParams(vmem_limit_bytes=40 << 20),
        name="sketch_gram",
    )(place[None], mixed, weight)

    total = keep + xor_send(send, mask_of(stages[0], 1), n_dev)
    for stage in stages[1:]:
        ways = 1 << len(stage)
        if ways == 1:
            continue
        parts = total.reshape(ways, total.shape[0] // ways, 8, lanes)
        got = [xor_send(parts[s], mask_of(stage, s), n_dev) for s in range(1, ways)]
        total = parts[0]
        for g in got:
            total = total + g

    def spread(total, stage):
        ways = 1 << len(stage)
        got = [xor_send(total, mask_of(stage, s), n_dev) for s in range(1, ways)]
        return jnp.concatenate([total] + got, axis=0) if got else total

    row_width = n // n_row
    col_width = n // n_grp
    cuts = [0, nb]
    tiles = head_tiles(nb, cuts[1], deep) if len(cuts) > 2 else 0

    def factor(p0, p1, own, state):
        last = p1 == nb
        store = [((p1 - p0) * TILE, n)] * 3
        work = 8 * 2 * n * n * TILE * (p1 - p0)
        return pl.pallas_call(
            functools.partial(factor_kernel, n, p0, p1, tiles),
            out_shape=(
                (jax.ShapeDtypeStruct((row_width, col_width), f32),)
                if last
                else tuple(jax.ShapeDtypeStruct(d, jnp.bfloat16) for d in store)
                + (jax.ShapeDtypeStruct((rows, TILE), f32),)
            ),
            in_specs=[smem] + [vmem] * (2 + len(state)),
            out_specs=(vmem,) * (1 if last else 4),
            scratch_shapes=[
                pltpu.VMEM((rows, own[0].shape[2]), f32),
                pltpu.VMEM((8, TILE), f32),
                pltpu.VMEM((TILE, TILE), f32),
            ]
            + ([pltpu.VMEM(d, jnp.bfloat16) for d in store] if last else []),
            compiler_params=pltpu.CompilerParams(vmem_limit_bytes=40 << 20),
            cost_estimate=pl.CostEstimate(flops=work, bytes_accessed=1 << 20, transcendentals=0),
            name="factor",
        )(jnp.stack([place, row_i, grp_i]), *own, *state)

    total = spread(total, stages[2])
    split_lanes = [0] + [tiles * TILE] * (len(cuts) > 2) + [lanes]
    shares = [spread(total[:, :, lo:hi], stages[1]) for lo, hi in zip(split_lanes, split_lanes[1:])]
    state = ()
    for p0, p1, share in zip(cuts, cuts[1:], shares):
        if state:
            share, state = lax.optimization_barrier((share, state))
        state = factor(p0, p1, (share, xor_send(share, mask_of(stages[0], 1), n_dev)), state)
    return state[0]


def local(panel_rows, sign_bits, sample_rows):
    rows_dev, n = panel_rows.shape
    n_row = lax.axis_size("row")
    n_grp = lax.axis_size("grp")
    n_dev = n_row * n_grp
    fits = (
        n % (2 * TILE) == 0
        and n_dev & (n_dev - 1) == 0
        and rows_dev & (rows_dev - 1) == 0
        and rows_dev % TILE == 0
        and 2 <= n_row
        and n_dev <= 64
        and rows_dev % (8 * n_dev) == 0
        and n_dev % 8 == 0
        and TILE % (n // n_row) == 0
        and n // n_row % 8 == 0
        and n // n_grp % TILE == 0
    )
    return (local_fast if fits else local_plain)(panel_rows, sign_bits, sample_rows)


def solution(mesh):
    return jax.shard_map(
        local,
        mesh=mesh,
        in_specs=(P(("row", "grp"), None), P(("row", "grp")), P()),
        out_specs=P("row", "grp"),
        check_vma=False,
    )
```

```python
import functools
import math

import jax
import jax.numpy as jnp
from jax import lax
from jax.experimental import pallas as pl
from jax.experimental.pallas import tpu as pltpu
from jax.sharding import PartitionSpec as P

AXES = ("row", "grp")
TILE = 128
f32 = jnp.float32


def hadamard(table_size, dtype):
    row_ids = lax.broadcasted_iota(jnp.int32, (table_size, table_size), 0)
    col_ids = lax.broadcasted_iota(jnp.int32, (table_size, table_size), 1)
    shared = row_ids & col_ids
    parity = jnp.zeros((table_size, table_size), jnp.int32)
    for bit_pos in range(table_size.bit_length() - 1):
        parity = parity ^ shared >> bit_pos & 1
    return (1 - 2 * parity).astype(dtype)


def mix_lead(exchanged):
    lead_table = hadamard(exchanged.shape[0], jnp.float32)
    return jnp.einsum("ab,bic->aic", lead_table, exchanged, precision=lax.Precision.HIGHEST)


def mix_grp(exchanged):
    return lax.all_to_all(mix_lead(exchanged), "grp", split_axis=0, concat_axis=2, tiled=True)


def local_plain(panel_rows, sign_bits, sample_rows):
    rows_dev, n_cols = panel_rows.shape
    n_row = lax.axis_size("row")
    n_grp = lax.axis_size("grp")
    flipped = panel_rows * (1 - 2 * sign_bits).astype(jnp.bfloat16)[:, None]
    local_table = hadamard(rows_dev, jnp.bfloat16)
    local_mix = jnp.dot(local_table, flipped, preferred_element_type=jnp.float32)
    grp_mixed = mix_grp(
        lax.all_to_all(local_mix[None], "grp", split_axis=2, concat_axis=0, tiled=True)
    )
    num_samples = sample_rows.shape[0]
    total_rows = rows_dev * n_row * n_grp
    norm_scale = 1.0 / math.sqrt(total_rows * num_samples)
    col_width = n_cols // n_grp
    col_start = lax.axis_index("grp") * col_width
    held = mix_lead(lax.all_to_all(grp_mixed, "row", split_axis=1, concat_axis=0, tiled=True))
    slice_width = held.shape[1]
    block_pos = lax.broadcasted_iota(jnp.int32, (n_row, slice_width), 0)
    inner_pos = lax.broadcasted_iota(jnp.int32, (n_row, slice_width), 1)
    held_ids = (
        (block_pos * n_grp + lax.axis_index("grp")) * rows_dev
        + lax.axis_index("row") * slice_width
        + inner_pos
    ).reshape(-1)
    found_pos = jnp.clip(jnp.searchsorted(sample_rows, held_ids), 0, num_samples - 1)
    is_sampled = jnp.take(sample_rows, found_pos) == held_ids
    held_flat = held.reshape(n_row * slice_width, n_cols)
    sketch_held = jnp.where(is_sampled[:, None], held_flat * norm_scale, 0.0).astype(jnp.bfloat16)
    shard_rows = lax.all_gather(sketch_held, "grp", axis=0, tiled=True)
    own_cols = lax.dynamic_slice_in_dim(shard_rows, col_start, col_width, 1)
    partial_value = lax.dot_general(
        shard_rows, own_cols, (((0,), (0,)), ((), ())), preferred_element_type=jnp.float32
    )
    gram_block = lax.psum_scatter(partial_value, "row", scatter_dimension=0, tiled=True)
    gathered = lax.all_gather(gram_block[None], ("row", "grp"), axis=0, tiled=True)
    gram_matrix = (
        gathered.reshape(n_row, n_grp, n_cols // n_row, col_width)
        .transpose(0, 2, 1, 3)
        .reshape(n_cols, n_cols)
    )
    lower_factor = jnp.linalg.cholesky(gram_matrix)
    row_width = n_cols // n_row
    return lax.dynamic_slice(
        lower_factor, (lax.axis_index("row") * row_width, col_start), (row_width, col_width)
    )


TA = (((0,), (0,)), ((), ()))
LEFT = (0, 0, 1, 0, 2, 1)
RIGHT = (0, 1, 0, 2, 0, 1)


def split(x):
    hi = x.astype(jnp.bfloat16)
    rest = x - hi.astype(f32)
    mid = rest.astype(jnp.bfloat16)
    return hi, mid, (rest - mid.astype(f32)).astype(jnp.bfloat16)


def mm6(a, b, ca, cb):
    lhs = jnp.concatenate([a[i] for i in LEFT], axis=ca)
    rhs = jnp.concatenate([b[i] for i in RIGHT], axis=cb)
    return lax.dot_general(lhs, rhs, (((ca,), (cb,)), ((), ())), preferred_element_type=f32)


def eliminate(X, first, zero):
    G = X.shape[0] // 8
    xs = [X[8 * g : 8 * g + 8, :] for g in range(G)]
    rid = lax.broadcasted_iota(jnp.int32, (8, TILE), 0)

    def full(v):
        return jnp.broadcast_to(v, (8, TILE))

    def col(h, at):
        return full(xs[h][:, first + at : first + at + 1])

    out = []
    D = [col(0, m) + zero for m in range(8)]
    for g in range(G):
        C = D
        more = g + 1 < G
        near = [col(g + 1, 8 * g + m) for m in range(8)] if more else None
        D = [col(g + 1, 8 * g + 8 + m) for m in range(8)] if more else None
        far = {h: [col(h, 8 * g + m) for m in range(8)] for h in range(g + 2, G)}
        o = jnp.zeros((8, TILE), f32)
        for j in range(0, 8, 2):
            a = full(C[j][j : j + 1, :])
            b = full(C[j][j + 1 : j + 2, :])
            c = full(C[j + 1][j + 1 : j + 2, :])
            det = a * c - b * b
            inv = 1.0 / det
            ws = {}
            for m in range(j + 2, 8):
                q0 = full(C[m][j : j + 1, :])
                q1 = full(C[m][j + 1 : j + 2, :])
                t0 = c * q0 - b * q1
                t1 = a * q1 - b * q0
                ws[m] = t0 * inv, t1 * inv
                C[m] = C[m] - (C[j] * t0 + C[j + 1] * t1) * inv
            if more:
                n0 = c * near[j] - b * near[j + 1]
                n1 = a * near[j + 1] - b * near[j]
                if j == 6:
                    for m in range(8):
                        D[m] = D[m] - (near[j] * full(n0[m : m + 1, :]) + near[j + 1] * full(n1[m : m + 1, :])) * inv
                else:
                    v0 = n0 * inv
                    v1 = n1 * inv
                    for m in range(8):
                        D[m] = D[m] - near[j] * full(v0[m : m + 1, :]) - near[j + 1] * full(v1[m : m + 1, :])
            r0 = full(xs[g][j : j + 1, :])
            r1 = full(xs[g][j + 1 : j + 2, :])
            t1 = a * r1 - b * r0
            u0 = (c * r0 - b * r1) * inv
            u1 = t1 * inv
            if j < 6:
                xs[g] = xs[g] - C[j] * u0 - C[j + 1] * u1
            if more:
                xs[g + 1] = xs[g + 1] - near[j] * u0 - near[j + 1] * u1
                for m, (w0, w1) in ws.items():
                    near[m] = near[m] - near[j] * w0 - near[j + 1] * w1
            for h, cols in far.items():
                xs[h] = xs[h] - cols[j] * u0 - cols[j + 1] * u1
                for m, (w0, w1) in ws.items():
                    cols[m] = cols[m] - cols[j] * w0 - cols[j + 1] * w1
            l0 = r0 * lax.rsqrt(a)
            l1 = t1 * lax.rsqrt(a * det)
            o = jnp.where(rid == j, l0, jnp.where(rid == j + 1, l1, o))
        out.append(o)
    return jnp.concatenate(out, axis=0)


def scales(S, off):
    lane = lax.broadcasted_iota(jnp.int32, S.shape, 1)
    row = lax.broadcasted_iota(jnp.int32, S.shape, 0)
    diag = jnp.where(lane == row + off, S, 0.0)
    down = jnp.broadcast_to(lax.rsqrt(jnp.sum(diag, axis=1, keepdims=True)), S.shape)
    half = (lane >= off) & (lane < off + S.shape[0])
    across = jnp.where(half[0:1], jnp.sum(diag, axis=0, keepdims=True), 1.0)
    root = lax.rsqrt(across)
    return down, root, across * root


def scaled(S, scale, off, other):
    down, root, _ = scale
    lane = lax.broadcasted_iota(jnp.int32, S.shape, 1)
    row = lax.broadcasted_iota(jnp.int32, S.shape, 0)
    half = (lane >= off) & (lane < off + S.shape[0])
    return jnp.where(half, S * (down * root), jnp.where(lane == row + other, down, 0.0))


def local_kernel(sign_ref, panel_ref, out_ref, signed):
    blocks = panel_ref.shape[0] // TILE

    @pl.when(pl.program_id(0) == 0)
    def _():
        table = hadamard(TILE, f32)
        for b in range(blocks):
            sign = 1 - 2 * sign_ref[:, b * TILE : (b + 1) * TILE]
            signed[b] = (table * sign.astype(f32)).astype(jnp.bfloat16)

    v = [
        jnp.dot(signed[b], panel_ref[b * TILE : (b + 1) * TILE, :], preferred_element_type=f32) for b in range(blocks)
    ]
    h = 1
    while h < blocks:
        w = list(v)
        for b in range(blocks):
            if not b & h:
                w[b] = v[b] + v[b | h]
                w[b | h] = v[b] - v[b | h]
        v = w
        h *= 2
    for b in range(blocks):
        out_ref[b * TILE : (b + 1) * TILE, :] = v[b]


def cells_of(nb):
    cells = []
    for k in range(nb):
        cells.append(("top", k))
        cells += [("full", k, j, i) for j in range(k + 1, nb) for i in range(2)]
        if k % 2 == 0:
            cells.append(("low", k // 2))
    return cells


def head_tiles(nb, panels, deep):
    cells = cells_of(nb)
    need = [c for c in cells if c[1] < panels and c[0] != "low" or c[0] == "low" and 2 * c[1] < panels]
    return -(-(1 + max(cells.index(c) for c in need)) // deep)


def slot(nb, deep, cell):
    at = cells_of(nb).index(cell)
    half = TILE // 2
    return slice(at % deep * half, (at % deep + 1) * half), slice(at // deep * TILE, (at // deep + 1) * TILE)


def sketch_gram_kernel(n_dev, me_ref, x_ref, m_ref, keep_ref, send_ref, s_ref, pack):
    n = x_ref.shape[2]
    nb = n // TILE
    per = x_ref.shape[1]

    def mix(c, _):
        cols = pl.ds(pl.multiple_of(c * TILE, TILE), TILE)
        for sub in range(per // 8):
            v = [x_ref[b, 8 * sub : 8 * sub + 8, cols] for b in range(n_dev)]
            h = 1
            while h < n_dev:
                w = list(v)
                for b in range(n_dev):
                    if not b & h:
                        w[b] = v[b] + v[b | h]
                        w[b | h] = v[b] - v[b | h]
                v = w
                h *= 2
            for b in range(0, n_dev, 2):
                r = (sub * n_dev + b) * 8
                pair = jnp.concatenate([v[b], v[b + 1]], axis=0) * m_ref[r : r + 16, :]
                s_ref[r : r + 16, cols] = pair.astype(jnp.bfloat16)
        return 0

    lax.fori_loop(0, nb, mix, 0)
    H = TILE // 2
    deep = pack.shape[0] // H
    lane = lax.broadcasted_iota(jnp.int32, (H, TILE), 1)
    even = None
    for k in range(nb):
        part = lax.dot_general(
            s_ref[:, k * TILE : (k + 1) * TILE],
            s_ref[:, k * TILE :],
            TA,
            preferred_element_type=f32,
        )
        pack[slot(nb, deep, ("top", k))] = part[:H, :TILE]
        for j in range(k + 1, nb):
            for i in range(2):
                cols = slice((j - k) * TILE, (j - k + 1) * TILE)
                pack[slot(nb, deep, ("full", k, j, i))] = part[i * H : (i + 1) * H, cols]
        if k % 2 == 0:
            even = part[H:, :TILE]
        else:
            odd = pltpu.roll(part[H:, :TILE], H, 1)
            pack[slot(nb, deep, ("low", k // 2))] = jnp.where(lane < H, odd, even)
    half = n_dev // 2
    me = me_ref[0]
    h = keep_ref.shape[1]

    def put(j, _):
        keep_ref[j] = pack[pl.ds(pl.multiple_of((j ^ me) * h, 8), h), :]
        send_ref[j] = pack[pl.ds(pl.multiple_of(((j + half) ^ me) * h, 8), h), :]
        return 0

    lax.fori_loop(0, half, put, 0)


def factor_kernel(n, p0, p1, head, pos_ref, own_ref, recv_ref, *refs):
    refs = list(refs)
    last = p1 == n // TILE
    old = [refs.pop(0) for _ in range(3)] if p0 else None
    kept = refs.pop(0) if p0 else None
    if last:
        out_ref = refs.pop(0)
        parts = refs[-3:]
    else:
        parts = [refs.pop(0) for _ in range(3)]
        keep_ref = refs.pop(0)
    pack, zref, turn = refs[:3]
    B = TILE
    H = B // 2
    nb = n // B
    half = own_ref.shape[0]
    h = own_ref.shape[1]
    me = pos_ref[0]

    def get(j, _):
        pack[pl.ds(pl.multiple_of((j ^ me) * h, 8), h), :] = own_ref[j]
        pack[pl.ds(pl.multiple_of(((j + half) ^ me) * h, 8), h), :] = recv_ref[j]
        return 0

    lax.fori_loop(0, half, get, 0)
    zref[...] = jnp.zeros((8, B), f32)
    lane = lax.broadcasted_iota(jnp.int32, (H, B), 1)
    row = lax.broadcasted_iota(jnp.int32, (H, B), 0)
    low = lane < H

    deep = pack.shape[0] // H

    def cell(*name):
        rows, lanes = slot(nb, deep, name)
        if p0 and lanes.start < head * B:
            return kept[rows, lanes.start - (head - 1) * B : lanes.stop - (head - 1) * B]
        base = head * B if p0 else 0
        return pack[rows, lanes.start - base : lanes.stop - base]

    def diagonal(k):
        low_part = cell("low", k // 2)
        return jnp.concatenate([cell("top", k), pltpu.roll(low_part, H, 1) if k % 2 else low_part], axis=0)

    def beside(k):
        rows = [jnp.concatenate([cell("full", k, j, i) for j in range(k + 1, nb)], axis=1) for i in range(2)]
        return jnp.concatenate(rows, axis=0)

    def above(k, cols):
        new = [u[: (k - p0) * B, cols] for u in parts]
        if not p0:
            return new
        if k == p0:
            return [u[:, cols] for u in old]
        return [jnp.concatenate([o[:, cols], u], axis=0) for o, u in zip(old, new)]

    def store(r, cols, value):
        value = split(value)
        for u, v in zip(parts, value):
            u[r - p0 * B : r - p0 * B + H, cols] = v
        return value

    def under(value, top):
        zero = jnp.zeros(value.shape, jnp.bfloat16)
        return [jnp.concatenate([zero, v] if top else [v, zero], axis=0) for v in split(value)]

    def gram_scales(k):
        tile = diagonal(k)
        return scales(tile[:H], 0), scales(tile[H:], H)

    upper, lower = gram_scales(p0)
    D = diagonal(p0)
    if p0:
        left = above(p0, slice(p0 * B, (p0 + 1) * B))
        D = D - mm6(left, left, 0, 0)
    for k in range(p0, p1):
        r = k * B
        here = slice(r, r + B)
        rest = slice(r + B, n)
        then = slice(r + B, r + 2 * B)
        tail = k < nb - 1
        X1 = scaled(D[:H], upper, 0, H)
        back1, back2 = upper[2], lower[2]
        scale2 = lower
        if k < p1 - 1:
            upper, lower = gram_scales(k + 1)
        if tail:
            R = beside(k)
            if k:
                R = R - mm6(above(k, here), above(k, rest), 0, 0)
            if k < p1 - 1:
                E = diagonal(k + 1)
                if k:
                    left = above(k, then)
                    E = E - mm6(left, left, 0, 0)
        F1 = eliminate(X1, 0, zref[...]) * back1
        f1 = split(F1)
        U1 = mm6(f1, under(D[:H], True), 1, 0)
        u12 = split(jnp.where(low, 0.0, U1))
        D2 = D[H:] - mm6(u12, u12, 0, 0)[H:]
        X2 = scaled(D2, scale2, H, 0)
        store(r, here, jnp.where(low, jnp.where(lane >= row, F1, 0.0), U1))
        if tail:
            P1 = mm6(f1, under(R[:H], True), 1, 0)
            first = store(r, rest, P1)
            R2 = R[H:] - mm6(u12, first, 0, 0)[H:]
            if k < p1 - 1:
                first = [v[:, :B] for v in first]
                E = E - mm6(first, first, 0, 0)
        F2 = eliminate(X2, H, zref[...]) * back2
        store(r + H, here, jnp.where(low | (lane - H < row), 0.0, F2))
        if tail:
            P2 = mm6(split(F2), under(R2, False), 1, 0)
            second = [v[:, :B] for v in store(r + H, rest, P2)]
            if k < p1 - 1:
                D = E - mm6(second, second, 0, 0)
    if not last:
        keep_ref[...] = pack[:, (head - 1) * B :]
        return
    row_width, col_width = out_ref.shape
    first_row = pos_ref[1] * row_width
    first_col = pos_ref[2] * col_width
    lane_tile = pl.multiple_of(first_row // B * B, B)
    inner = pl.multiple_of(first_row % B, 8)
    for c in range(col_width // B):
        rb = first_col // B + c

        def take(src, block):
            where = (pl.ds(pl.multiple_of(block * B, B), B), pl.ds(lane_tile, B))
            hi, mid, tiny = (u[where].astype(f32) for u in src)
            turn[...] = ((tiny + mid) + hi).T

        if p0:
            pl.when(rb < p0)(lambda: take(old, jnp.minimum(rb, p0 - 1)))
        pl.when(rb >= p0)(lambda: take(parts, jnp.clip(rb - p0, 0, nb - p0 - 1)))
        i = first_row + lax.broadcasted_iota(jnp.int32, (row_width, B), 0)
        j = first_col + c * B + lax.broadcasted_iota(jnp.int32, (row_width, B), 1)
        out_ref[:, c * B : (c + 1) * B] = jnp.where(j <= i, turn[pl.ds(inner, row_width), :], 0.0)


def xor_send(value, mask, n_dev):
    return lax.ppermute(value, AXES, [(d, d ^ mask) for d in range(n_dev)])


def local_fast(panel_rows, sign_bits, sample_rows):
    rows_dev, n = panel_rows.shape
    n_row = lax.axis_size("row")
    n_grp = lax.axis_size("grp")
    n_dev = n_row * n_grp
    per = rows_dev // n_dev
    num_samples = sample_rows.shape[0]
    norm_scale = 1.0 / math.sqrt(rows_dev * n_dev * num_samples)
    row_i = lax.axis_index("row")
    grp_i = lax.axis_index("grp")
    lin = row_i * n_grp + grp_i

    vmem = pl.BlockSpec(memory_space=pltpu.VMEM)
    smem = pl.BlockSpec(memory_space=pltpu.SMEM)
    width = math.gcd(n, 4 * TILE)
    local_mix = pl.pallas_call(
        local_kernel,
        grid=(n // width,),
        out_shape=jax.ShapeDtypeStruct((rows_dev, n), f32),
        in_specs=[
            pl.BlockSpec((1, rows_dev), lambda c: (0, 0)),
            pl.BlockSpec((rows_dev, width), lambda c: (0, c)),
        ],
        out_specs=pl.BlockSpec((rows_dev, width), lambda c: (0, c)),
        scratch_shapes=[pltpu.VMEM((rows_dev // TILE, TILE, TILE), jnp.bfloat16)],
        compiler_params=pltpu.CompilerParams(vmem_limit_bytes=60 << 20),
        name="local_mix",
    )(sign_bits[None], panel_rows)
    mixed = lax.all_to_all(local_mix, AXES, split_axis=0, concat_axis=0, tiled=True)
    mixed = mixed.reshape(n_dev, per, n)

    r = lax.iota(jnp.int32, rows_dev)
    held_ids = (r // 8 % n_dev) * rows_dev + lin * per + r // (8 * n_dev) * 8 + r % 8
    is_sampled = jnp.any(held_ids[:, None] == sample_rows[None, :], axis=1)
    weight = jnp.where(is_sampled, norm_scale, 0.0).astype(f32)
    weight = jnp.broadcast_to(weight[:, None], (rows_dev, TILE))

    grp_bits = [1 << b for b in range(n_grp.bit_length() - 1)]
    row_bits = [n_grp << b for b in range(n_row.bit_length() - 1)]
    stages = [row_bits[:1], row_bits[1:2] + grp_bits, row_bits[2:]]
    order = [bit for stage in stages for bit in reversed(stage)]
    place = jnp.int32(0)
    for bit in order:
        place = place * 2 + (lin & bit) // bit

    def mask_of(stage, step):
        return sum(bit for pos, bit in enumerate(stage) if step >> pos & 1)

    nb = n // TILE
    rows = 8 * n_dev
    deep = rows // (TILE // 2)
    lanes = -(-len(cells_of(nb)) // deep) * TILE
    half = n_dev // 2
    piece = jax.ShapeDtypeStruct((half, 8, lanes), f32)
    keep, send = pl.pallas_call(
        functools.partial(sketch_gram_kernel, n_dev),
        out_shape=(piece, piece),
        in_specs=[smem, vmem, vmem],
        out_specs=(vmem, vmem),
        scratch_shapes=[pltpu.VMEM((rows_dev, n), jnp.bfloat16), pltpu.VMEM((rows, lanes), f32)],
        compiler_params=pltpu.CompilerParams(vmem_limit_bytes=40 << 20),
        name="sketch_gram",
    )(place[None], mixed, weight)

    total = keep + xor_send(send, mask_of(stages[0], 1), n_dev)
    for stage in stages[1:]:
        ways = 1 << len(stage)
        if ways == 1:
            continue
        parts = total.reshape(ways, total.shape[0] // ways, 8, lanes)
        got = [xor_send(parts[s], mask_of(stage, s), n_dev) for s in range(1, ways)]
        total = parts[0]
        for g in got:
            total = total + g

    def spread(total, stage):
        ways = 1 << len(stage)
        got = [xor_send(total, mask_of(stage, s), n_dev) for s in range(1, ways)]
        return jnp.concatenate([total] + got, axis=0) if got else total

    row_width = n // n_row
    col_width = n // n_grp
    cuts = [0, nb]
    tiles = head_tiles(nb, cuts[1], deep) if len(cuts) > 2 else 0

    def factor(p0, p1, own, state):
        last = p1 == nb
        store = [((p1 - p0) * TILE, n)] * 3
        work = 8 * 2 * n * n * TILE * (p1 - p0)
        return pl.pallas_call(
            functools.partial(factor_kernel, n, p0, p1, tiles),
            out_shape=(
                (jax.ShapeDtypeStruct((row_width, col_width), f32),)
                if last
                else tuple(jax.ShapeDtypeStruct(d, jnp.bfloat16) for d in store)
                + (jax.ShapeDtypeStruct((rows, TILE), f32),)
            ),
            in_specs=[smem] + [vmem] * (2 + len(state)),
            out_specs=(vmem,) * (1 if last else 4),
            scratch_shapes=[
                pltpu.VMEM((rows, own[0].shape[2]), f32),
                pltpu.VMEM((8, TILE), f32),
                pltpu.VMEM((TILE, TILE), f32),
            ]
            + ([pltpu.VMEM(d, jnp.bfloat16) for d in store] if last else []),
            compiler_params=pltpu.CompilerParams(vmem_limit_bytes=40 << 20),
            cost_estimate=pl.CostEstimate(flops=work, bytes_accessed=1 << 20, transcendentals=0),
            name="factor",
        )(jnp.stack([place, row_i, grp_i]), *own, *state)

    total = spread(total, stages[2])
    split_lanes = [0] + [tiles * TILE] * (len(cuts) > 2) + [lanes]
    shares = [spread(total[:, :, lo:hi], stages[1]) for lo, hi in zip(split_lanes, split_lanes[1:])]
    state = ()
    for p0, p1, share in zip(cuts, cuts[1:], shares):
        if state:
            share, state = lax.optimization_barrier((share, state))
        state = factor(p0, p1, (share, xor_send(share, mask_of(stages[0], 1), n_dev)), state)
    return state[0]


def local(panel_rows, sign_bits, sample_rows):
    rows_dev, n = panel_rows.shape
    n_row = lax.axis_size("row")
    n_grp = lax.axis_size("grp")
    n_dev = n_row * n_grp
    fits = (
        n % (2 * TILE) == 0
        and n_dev & (n_dev - 1) == 0
        and rows_dev & (rows_dev - 1) == 0
        and rows_dev % TILE == 0
        and 2 <= n_row
        and n_dev <= 64
        and rows_dev % (8 * n_dev) == 0
        and n_dev % 8 == 0
        and TILE % (n // n_row) == 0
        and n // n_row % 8 == 0
        and n // n_grp % TILE == 0
    )
    return (local_fast if fits else local_plain)(panel_rows, sign_bits, sample_rows)


def solution(mesh):
    return jax.shard_map(
        local,
        mesh=mesh,
        in_specs=(P(("row", "grp"), None), P(("row", "grp")), P()),
        out_specs=P("row", "grp"),
        check_vma=False,
    )
```
